32 devices in a mesh: rows: 4 (over z), cols: 8 (over y, x, core).
Axes of the slice: x: 2, y: 2, z: 4, core: 2. Of those that a mesh axis runs over, the one named last changes fastest.
Arguments:
- left_fine: bfloat16 [128, 1024, 128], P('rows', 'cols'), may hold values from -40 to 40
- right_fine: bfloat16 [128, 1024, 128], P('rows', 'cols'), may hold values from -40 to 40
- left_coarse: bfloat16 [32, 256, 128], P('rows', 'cols'), may hold values from -40 to 40
- right_coarse: bfloat16 [32, 256, 128], P('rows', 'cols'), may hold values from -40 to 40
- candidates: int32 [8, 32, 4], P(None, 'rows'), may hold values from 0 to 7, all different within a row; in each aligned block of 8 rows (0 to 7, 8 to 15, ..., all dimensions but the last counted through in order) at most 8 rows name the same one
- counts: int32 [8, 32], P(None, 'rows'), may hold values from 1 to 4
- query_weight: bfloat16 [128, 128], replicated, may hold values from -1 to 1
- key_weight: bfloat16 [128, 128], replicated, may hold values from -1 to 1
- value_weight: bfloat16 [128, 128], replicated, may hold values from -0.5 to 0.5
- out_weight: bfloat16 [128, 128], replicated, may hold values from -0.5 to 0.5
- norm_gain: float32 [128], replicated, may hold values from 0.5 to 1.5
Outputs:
- fine_features: bfloat16 [128, 1024, 128], P('rows', 'cols')
- coarse_prior: bfloat16 [32, 256, 128], P('rows', 'cols')
The draws below stay inside these ranges and needn't reach their ends.
Inputs may be any that keep to these rules, and one draw needn't show every extreme that they name: `candidates`: each list names 4 different right blocks; entries at k >= counts are not used. For one left block, within the 8 bands of one index of rows (aligned groups of bands), no right block is named more than 8 times, and in some groups one is named exactly 8 times.
All inputs are finite; a program needn't handle non-finite values.
Results may differ from the reference program's by a relative error of at most 0.01.
Values may be sent and summed in bfloat16 or wider, within the bound.
A program may use at most 192 MiB of HBM per device.

```python
import math
import jax
import jax.numpy as jnp
import numpy as np
from jax import lax

FEAT = 128
HEADS = 8
HEAD_DIM = 16
BLOCK = 128
BAND = 4
CANDS = 4
BANDS_DEV = 8
ROWS_FINE = 128
COLS_FINE = 1024
ROWS_COARSE = 32
COLS_COARSE = 256
BANDS = 32
CAP = 8
N_COLS = 8


def background(key, salt, shape):
    values = jnp.clip(jax.random.normal(jax.random.fold_in(key, salt), shape, jnp.float32), -4.0, 4.0)
    return values


def draw_left_fine(key, part):
    values = background(key, 31, (ROWS_FINE, COLS_FINE, FEAT))
    return values.astype(jnp.bfloat16)


def draw_right_fine(key, part):
    values = background(key, 33, (ROWS_FINE, COLS_FINE, FEAT))
    return values.astype(jnp.bfloat16)


def draw_left_coarse(key, part):
    values = background(key, 35, (ROWS_COARSE, COLS_COARSE, FEAT))
    return values.astype(jnp.bfloat16)


def draw_right_coarse(key, part):
    values = background(key, 37, (ROWS_COARSE, COLS_COARSE, FEAT))
    return values.astype(jnp.bfloat16)


def weight_base(key, salt):
    values = jnp.clip(jax.random.normal(jax.random.fold_in(key, salt), (FEAT, FEAT), jnp.float32), -4.0, 4.0)
    return values / jnp.sqrt(jnp.float32(FEAT))


def draw_query_weight(key, part):
    return weight_base(key, 51).astype(jnp.bfloat16)


def draw_key_weight(key, part):
    jitter = weight_base(key, 52)
    values = jitter
    return values.astype(jnp.bfloat16)


def with_ends(entries, stream_key, low, high):
    dims = entries.shape
    place = [jax.random.randint(jax.random.fold_in(stream_key, axis), (), 0, dims[axis]) for axis in range(len(dims))]
    entries = entries.at[tuple(place)].set(low)
    longest = dims.index(max(dims))
    place[longest] = (place[longest] + 1) % dims[longest]
    return entries.at[tuple(place)].set(high)


def shared_out(own_key, own, number, rows, number_of, top, reach, lean):
    order = jax.random.permutation(own_key, number_of)
    packed, common = portions_of(number_of, rows * top, reach, lean, True), portions_of(number_of, rows * top, reach, lean, False)
    places = jnp.arange(number_of)

    def named(tallies, rotation):
        used = int((tallies > 0).sum())
        fixed = max(1, used // 4)
        passed = fixed + (places - fixed + rotation * (used - fixed)) % max(1, number_of - fixed)
        return jnp.zeros((number_of,), jnp.int32).at[order[jnp.where(places < fixed, places, passed)]].set(jnp.asarray(tallies, jnp.int32))

    tallies = jnp.where(number % 4 == 0, named(packed, number // 4), named(common, number - number // 4 - 1))
    mixed = jax.random.permutation(jax.random.fold_in(own, 3), number_of)
    giver, receiver = mixed[0:number_of // 2 * 2:2], mixed[1:number_of // 2 * 2:2]
    room = jnp.minimum(tallies[giver] - 1, reach - tallies[receiver]) // 2
    room = jnp.where((giver == order[0]) | (receiver == order[0]) | (tallies[receiver] == 0), 0, jnp.maximum(room, 0))
    passed = jax.random.randint(jax.random.fold_in(own, 4), (number_of // 2,), 0, 1 << 20) % (room + 1)
    tallies = tallies.at[giver].add(-passed).at[receiver].add(passed)
    labels = jnp.searchsorted(jnp.cumsum(tallies), jnp.arange(rows * top), side="right").astype(jnp.int32)
    table = labels.reshape(top, rows).T
    table = table[jax.random.permutation(jax.random.fold_in(own, 1), rows)]
    rotation = jax.random.randint(jax.random.fold_in(own, 2), (rows, 1), 0, top)
    return jnp.take_along_axis(table, (jnp.arange(top)[None, :] + rotation) % top, axis=1)


def portions_of(amount, total, limit, skew, full):
    weights = [(1 << 20) // math.isqrt(grade ** skew) + 1 for grade in range(1, amount + 1)]
    largest = limit if full else min(limit, max(-(-total // amount), total * weights[0] // sum(weights)))
    least = 1 if total - largest >= amount - 1 else 0
    given, surplus = [largest] + [least] * (amount - 1), total - largest - least * (amount - 1)
    while surplus > 0:
        free = [i for i in range(1, amount) if given[i] < largest] or [i for i in range(1, amount) if given[i] < limit]
        pool, remaining = sum([weights[i] for i in free]), surplus
        for i in free:
            extra = min(limit - given[i], max(1, remaining * weights[i] // pool), surplus)
            given[i] = given[i] + extra
            surplus = surplus - extra
    return np.array(given)


def gaussian(own_key, extent, scale, reach, kind=jnp.bfloat16):
    result = jax.random.normal(own_key, extent, jnp.float32) * scale
    return jnp.minimum(jnp.maximum(result, -reach), reach).astype(kind)


def setup_inputs(seed: int = 0) -> dict:
    seeds = jax.random.split(jax.random.key(seed), 12)
    left_fine = draw_left_fine(jax.random.fold_in(seeds[11], 71), 0)
    right_fine = draw_right_fine(jax.random.fold_in(seeds[11], 71), 0)
    left_coarse = draw_left_coarse(jax.random.fold_in(seeds[11], 71), 0)
    right_coarse = draw_right_coarse(jax.random.fold_in(seeds[11], 71), 0)
    candidates_keys = jax.random.split(jax.random.fold_in(seeds[4], 1), N_COLS * BANDS // BANDS_DEV)
    candidates_turns = jax.random.permutation(jax.random.fold_in(seeds[4], 3), N_COLS * BANDS // BANDS_DEV)
    candidates = jax.vmap(lambda own, number: shared_out(jax.random.fold_in(seeds[4], 2), own, number, BANDS_DEV, N_COLS, CANDS, CAP, 2))(candidates_keys, candidates_turns).reshape((N_COLS, BANDS, CANDS))
    counts = with_ends(jax.random.randint(seeds[5], (N_COLS, BANDS), 1, CANDS + 1), jax.random.fold_in(seeds[5], 1), 1, CANDS).astype(jnp.int32)
    query_weight = draw_query_weight(jax.random.fold_in(seeds[11], 71), 0)
    key_weight = draw_key_weight(jax.random.fold_in(seeds[11], 71), 0)
    value_weight = gaussian(seeds[8], (FEAT, FEAT), FEAT ** -0.5, 0.5)
    out_weight = gaussian(seeds[9], (FEAT, FEAT), FEAT ** -0.5, 0.5)
    norm_gain = jnp.clip(1.0 + 0.1 * jax.random.normal(seeds[10], (FEAT,), jnp.float32), 0.5, 1.5)
    return {"left_fine": left_fine, "right_fine": right_fine, "left_coarse": left_coarse, "right_coarse": right_coarse, "candidates": candidates, "counts": counts, "query_weight": query_weight, "key_weight": key_weight, "value_weight": value_weight, "out_weight": out_weight, "norm_gain": norm_gain}


EPSILON = 1e-05

def layer_norm(values, norm_gain):
    average = lax.optimization_barrier(jnp.mean(values, axis=-1, keepdims=True))
    centred = values - average
    spread = lax.optimization_barrier(jnp.mean(centred * centred, axis=-1, keepdims=True))
    return centred * lax.rsqrt(spread + EPSILON) * norm_gain

def project(values, weight):
    flat_rows = values.reshape(-1, values.shape[-1])
    product = jnp.dot(flat_rows, weight, preferred_element_type=jnp.float32)
    return product.astype(jnp.bfloat16).reshape(values.shape[:-1] + (weight.shape[1],))

def split_heads(values):
    return values.reshape(values.shape[:-1] + (HEADS, HEAD_DIM)).astype(jnp.float32)

def blend(values, axis_pos, before_rows, after_rows):
    stacked = jnp.stack([0.375 * before_rows + 0.625 * values, 0.125 * before_rows + 0.875 * values, 0.875 * values + 0.125 * after_rows, 0.625 * values + 0.375 * after_rows], axis=axis_pos + 1)
    new_shape = values.shape[:axis_pos] + (4 * values.shape[axis_pos],) + values.shape[axis_pos + 1:]
    return stacked.reshape(new_shape)

def reference(left_fine, right_fine, left_coarse, right_coarse, candidates, counts, query_weight, key_weight, value_weight, out_weight, norm_gain):
    scale_factor = 1.0 / math.sqrt(HEAD_DIM)
    coarse_query = project(left_coarse, query_weight)
    coarse_key = project(right_coarse, key_weight)
    coarse_value = project(right_coarse, value_weight)

    def coarse_row(inputs):
        row_query, row_key, row_value = inputs
        scores = jnp.einsum('qhd,khd->hqk', split_heads(row_query), split_heads(row_key)) * scale_factor
        weights = jax.nn.softmax(scores, axis=-1).astype(jnp.bfloat16)
        mixture = jnp.einsum('hqk,khd->qhd', weights.astype(jnp.float32), split_heads(row_value))
        return mixture.astype(jnp.bfloat16).reshape(row_query.shape)
    coarse_attn = lax.map(coarse_row, (coarse_query, coarse_key, coarse_value))
    coarse_mix = jnp.dot(coarse_attn.reshape(-1, FEAT), out_weight, preferred_element_type=jnp.float32)
    coarse_mix = coarse_mix.reshape(left_coarse.shape)
    coarse_prior = layer_norm(left_coarse.astype(jnp.float32) + coarse_mix, norm_gain).astype(jnp.bfloat16)
    prior_float = coarse_prior.astype(jnp.float32)

    def fine_band(inputs):
        band_index, left_rows, right_rows, band_cands, band_counts = inputs
        middle_row = lax.dynamic_index_in_dim(prior_float, band_index, 0, keepdims=True)
        lower_row = lax.dynamic_index_in_dim(prior_float, jnp.maximum(band_index - 1, 0), 0, keepdims=True)
        upper_row = lax.dynamic_index_in_dim(prior_float, jnp.minimum(band_index + 1, ROWS_COARSE - 1), 0, keepdims=True)
        row_up = blend(middle_row, 0, lower_row, upper_row)
        left_cols = jnp.concatenate([row_up[:, :1], row_up[:, :-1]], axis=1)
        right_cols = jnp.concatenate([row_up[:, 1:], row_up[:, -1:]], axis=1)
        upsampled = blend(row_up, 1, left_cols, right_cols)
        query_in = (left_rows.astype(jnp.float32) + upsampled).astype(jnp.bfloat16)
        queries = project(query_in, query_weight).reshape(BAND, N_COLS, BLOCK, FEAT)
        keys_band = project(right_rows, key_weight).reshape(BAND, N_COLS, BLOCK, FEAT)
        values_band = project(right_rows, value_weight).reshape(BAND, N_COLS, BLOCK, FEAT)
        picked_keys = keys_band[:, band_cands]
        picked_values = values_band[:, band_cands]
        scores = jnp.einsum('rbqhd,rbckhd->brhqck', split_heads(queries), split_heads(picked_keys)) * scale_factor
        usable = jnp.arange(CANDS, dtype=jnp.int32)[None, :] < band_counts[:, None]
        scores = jnp.where(usable[:, None, None, None, :, None], scores, -1e+30)
        flat_scores = scores.reshape(scores.shape[:4] + (CANDS * BLOCK,))
        weights = jax.nn.softmax(flat_scores, axis=-1).astype(jnp.bfloat16).reshape(scores.shape)
        mixture = jnp.einsum('brhqck,rbckhd->rbqhd', weights.astype(jnp.float32), split_heads(picked_values))
        mixture = mixture.astype(jnp.bfloat16).reshape(BAND * COLS_FINE, FEAT)
        fine_mix = jnp.dot(mixture, out_weight, preferred_element_type=jnp.float32).reshape(BAND, COLS_FINE, FEAT)
        return layer_norm(query_in.astype(jnp.float32) + fine_mix, norm_gain).astype(jnp.bfloat16)
    band_ids = jnp.arange(BANDS, dtype=jnp.int32)
    fine_out = lax.map(fine_band, (band_ids, left_fine.reshape(BANDS, BAND, COLS_FINE, FEAT), right_fine.reshape(BANDS, BAND, COLS_FINE, FEAT), jnp.transpose(candidates, (1, 0, 2)), jnp.transpose(counts, (1, 0))))
    return (fine_out.reshape(ROWS_FINE, COLS_FINE, FEAT), coarse_prior)
```

```python
import functools
import math

import jax
import jax.numpy as jnp
import numpy as np
from jax import lax
from jax.experimental import pallas as pl
from jax.experimental.pallas import tpu as pltpu
from jax.sharding import PartitionSpec as P

HEADS = 8
HEAD_DIM = 16
BLOCK = 128
BAND = 4
EPSILON = 1e-05
PAIRS = HEADS // 2
PAIR_ROWS = 3 * HEAD_DIM
KEY_SCALE = math.log2(math.e) / math.sqrt(HEAD_DIM)
BF16 = jnp.bfloat16
F32 = jnp.float32


def nt(a, b):
    return lax.dot_general(a, b, (((1,), (1,)), ((), ())), preferred_element_type=F32)


def tn(a, b):
    return lax.dot_general(a, b, (((0,), (0,)), ((), ())), preferred_element_type=F32)


def nn(a, b):
    return jnp.dot(a, b, preferred_element_type=F32)


def layer_norm(values, norm_gain):
    average = jnp.mean(values, axis=-1, keepdims=True)
    centred = values - average
    spread = jnp.mean(centred * centred, axis=-1, keepdims=True)
    return centred * lax.rsqrt(spread + EPSILON) * norm_gain


def upsample_matrix(cols, pitch):
    taps = np.array(
        [[0.375, 0.625, 0.0], [0.125, 0.875, 0.0], [0.0, 0.875, 0.125], [0.0, 0.625, 0.375]]
    )
    out = np.zeros((BAND, cols, 4, 3, pitch), np.float32)
    for c in range(cols):
        for t in range(4):
            for d in range(3):
                out[:, c, t, :, c + d] = taps[:, :] * taps[t, d]
    return out.reshape(BAND * cols * 4, 3 * pitch)


def value_rows(value_weight):
    rows = value_weight.T.reshape(PAIRS, 2 * HEAD_DIM, -1)
    rows = jnp.concatenate([rows, jnp.zeros_like(rows[:, :HEAD_DIM])], axis=1)
    return rows.reshape(PAIRS * PAIR_ROWS, -1)


def ones_rows():
    rows = np.zeros((PAIRS, PAIR_ROWS, BLOCK), np.float32)
    rows[:, 2 * HEAD_DIM :] = 1.0
    return rows.reshape(PAIRS * PAIR_ROWS, BLOCK)


def attend(keys, values, spread_ref):
    parts = []
    width = spread_ref.shape[1] // HEADS
    for pair in range(PAIRS):
        scores = nn(keys, spread_ref[:, pair * 2 * width : (pair + 1) * 2 * width])
        top = jnp.max(scores, axis=0, keepdims=True)
        weights = jnp.exp2((scores - top).astype(BF16))
        mix = nn(values[pair * PAIR_ROWS : (pair + 1) * PAIR_ROWS], weights)
        total = mix[2 * HEAD_DIM : 2 * HEAD_DIM + 1]
        inverse = 1.0 / total
        parts.append(mix[:HEAD_DIM, :width] * inverse[:, :width])
        parts.append(mix[HEAD_DIM : 2 * HEAD_DIM, width:] * inverse[:, width:])
    return jnp.concatenate(parts, axis=0).astype(BF16)


def fine_kernel(
    cand_ref,
    count_ref,
    left_ref,
    ext_ref,
    up_ref,
    wq_ref,
    wk_ref,
    wv_ref,
    ones_ref,
    wo_ref,
    gain_ref,
    *refs,
):
    list_length = len(refs) - 4
    cand_refs = refs[:list_length]
    out_ref, query_ref, spread_ref, mix_ref = refs[list_length:]
    band = pl.program_id(0)
    feat = wq_ref.shape[0]

    @pl.when(band == 0)
    def _():
        spread_ref[...] = jnp.zeros_like(spread_ref)

    pitch = ext_ref.shape[1]
    coarse = jnp.concatenate([ext_ref[band + i] for i in range(3)], axis=0)
    up = nn(up_ref[...], coarse)
    query_in = (left_ref[...].reshape(BAND * BLOCK, feat).astype(F32) + up).astype(BF16)
    query_ref[...] = nt(wq_ref[...], query_in).astype(BF16)

    for used in range(1, list_length + 1):

        @pl.when(count_ref[band] == used)
        def _():
            def row(r, carry):
                keys, values = [], []
                for k in range(used):
                    block = cand_refs[k][0, r]
                    keys.append((nn(block, wk_ref[...]) * KEY_SCALE).astype(BF16))
                    values.append((nt(wv_ref[...], block) + ones_ref[...]).astype(BF16))
                keys = jnp.concatenate(keys, axis=0)
                values = jnp.concatenate(values, axis=1)
                start = pl.multiple_of(r * BLOCK, BLOCK)
                for h in range(HEADS):
                    rows = slice(h * HEAD_DIM, (h + 1) * HEAD_DIM)
                    spread_ref[rows, h * BLOCK : (h + 1) * BLOCK] = query_ref[
                        rows, pl.ds(start, BLOCK)
                    ]
                mix_ref[:, pl.ds(start, BLOCK)] = attend(keys, values, spread_ref)
                return carry

            lax.fori_loop(0, BAND, row, 0)

    mixed = tn(mix_ref[...], wo_ref[...])
    out = layer_norm(query_in.astype(F32) + mixed, gain_ref[...])
    out_ref[...] = out.astype(BF16).reshape(out_ref.shape)


def fine_stage(left_fine, gathered, ext, own_lists, own_counts, wq, wk, wv, wo, gain):
    rows, cols, feat = left_fine.shape
    bands = rows // BAND
    length = own_lists.shape[1]
    up = jnp.asarray(upsample_matrix(cols // 4, ext.shape[1]), BF16)
    ones = jnp.asarray(ones_rows(), F32)
    vrows = value_rows(wv)

    def whole(shape):
        return pl.BlockSpec(shape, lambda g, c, n: (0,) * len(shape))

    def picked(k):
        return pl.BlockSpec((1, BAND, cols, feat), lambda g, c, n: (c[g * length + k], g, 0, 0))

    return pl.pallas_call(
        fine_kernel,
        grid_spec=pltpu.PrefetchScalarGridSpec(
            num_scalar_prefetch=2,
            grid=(bands,),
            in_specs=[
                pl.BlockSpec((BAND, cols, feat), lambda g, c, n: (g, 0, 0)),
                whole(ext.shape),
                whole(up.shape),
                whole(wq.shape),
                whole(wk.shape),
                whole(vrows.shape),
                whole(ones.shape),
                whole(wo.shape),
                whole((1, feat)),
            ]
            + [picked(k) for k in range(length)],
            out_specs=pl.BlockSpec((BAND, cols, feat), lambda g, c, n: (g, 0, 0)),
            scratch_shapes=[
                pltpu.VMEM((feat, BAND * BLOCK), BF16),
                pltpu.VMEM((feat, HEADS * BLOCK), BF16),
                pltpu.VMEM((feat, BAND * BLOCK), BF16),
            ],
        ),
        out_shape=jax.ShapeDtypeStruct(left_fine.shape, BF16),
        name="fine_stage",
    )(
        own_lists.reshape(-1),
        own_counts,
        left_fine,
        ext,
        up,
        wq.T,
        wk,
        vrows,
        ones,
        wo,
        gain.reshape(1, feat),
        *([gathered] * length),
    )


def extended(block, sides, width):
    for axis, dim in sides:
        count = lax.axis_size(axis)
        forward = [(i, i + 1) for i in range(count - 1)]
        backward = [(target, source) for source, target in forward]
        low = lax.ppermute(
            lax.slice_in_dim(block, block.shape[dim] - width, None, axis=dim), axis, forward
        )
        high = lax.ppermute(lax.slice_in_dim(block, 0, width, axis=dim), axis, backward)
        block = jnp.concatenate([low, block, high], axis=dim)
    return block


def project(values, weight):
    flat_rows = values.reshape(-1, values.shape[-1])
    product = jnp.dot(flat_rows, weight, preferred_element_type=jnp.float32)
    return product.astype(jnp.bfloat16).reshape(values.shape[:-1] + (weight.shape[1],))


def split_heads(values):
    return values.reshape(values.shape[:-1] + (HEADS, HEAD_DIM))


def body(
    left_fine,
    right_fine,
    left_coarse,
    right_coarse,
    candidates,
    counts,
    query_weight,
    key_weight,
    value_weight,
    out_weight,
    norm_gain,
):
    feat = left_fine.shape[-1]
    coarse_rows, coarse_cols = left_coarse.shape[:2]
    coarse_query = project(left_coarse, query_weight)
    coarse_all = lax.all_gather(right_coarse, "cols", axis=1, tiled=True)
    gathered = lax.all_gather(right_fine, "cols", axis=0, tiled=False)
    scores = jnp.einsum(
        "rqhd,rkhd->rhqk",
        split_heads(coarse_query),
        split_heads(project(coarse_all, key_weight)),
        preferred_element_type=jnp.float32,
    ) / math.sqrt(HEAD_DIM)
    weights = jax.nn.softmax(scores, axis=-1).astype(jnp.bfloat16)
    mixture = jnp.einsum(
        "rhqk,rkhd->rqhd",
        weights,
        split_heads(project(coarse_all, value_weight)),
        preferred_element_type=jnp.float32,
    ).astype(jnp.bfloat16)
    coarse_mix = jnp.dot(mixture.reshape(-1, feat), out_weight, preferred_element_type=jnp.float32)
    coarse_mix = coarse_mix.reshape(coarse_rows, coarse_cols, feat)
    coarse_prior = layer_norm(left_coarse.astype(jnp.float32) + coarse_mix, norm_gain).astype(
        jnp.bfloat16
    )
    padded = extended(coarse_prior, (("rows", 0), ("cols", 1)), 1)
    row_first = lax.axis_index("rows") == 0
    row_final = lax.axis_index("rows") == lax.axis_size("rows") - 1
    col_first = lax.axis_index("cols") == 0
    col_final = lax.axis_index("cols") == lax.axis_size("cols") - 1
    padded = padded.at[0].set(jnp.where(row_first, padded[1], padded[0]))
    padded = padded.at[-1].set(jnp.where(row_final, padded[-2], padded[-1]))
    padded = padded.at[:, 0].set(jnp.where(col_first, padded[:, 1], padded[:, 0]))
    padded = padded.at[:, -1].set(jnp.where(col_final, padded[:, -2], padded[:, -1]))
    pitch = -(-padded.shape[1] // 16) * 16
    padded = jnp.pad(padded, ((0, 0), (0, pitch - padded.shape[1]), (0, 0)))
    my_block = lax.axis_index("cols")
    own_lists = lax.dynamic_index_in_dim(candidates, my_block, 0, keepdims=False)
    own_counts = lax.dynamic_index_in_dim(counts, my_block, 0, keepdims=False)
    fine_features = fine_stage(
        left_fine,
        gathered,
        padded,
        own_lists,
        own_counts,
        query_weight,
        key_weight,
        value_weight,
        out_weight,
        norm_gain,
    )
    return (fine_features, coarse_prior)


def solution(mesh):
    return jax.shard_map(
        body,
        mesh=mesh,
        in_specs=(
            P("rows", "cols", None),
            P("rows", "cols", None),
            P("rows", "cols", None),
            P("rows", "cols", None),
            P(None, "rows", None),
            P(None, "rows"),
            P(),
            P(),
            P(),
            P(),
            P(),
        ),
        out_specs=(P("rows", "cols", None), P("rows", "cols", None)),
        check_vma=False,
    )
```

```python
import functools
import math

import jax
import jax.numpy as jnp
import numpy as np
from jax import lax
from jax.experimental import pallas as pl
from jax.experimental.pallas import tpu as pltpu
from jax.sharding import PartitionSpec as P

HEADS = 8
HEAD_DIM = 16
BLOCK = 128
BAND = 4
EPSILON = 1e-05
PAIRS = HEADS // 2
EDGE = 16
EARLY = 4
LEAD = 3
MESH = pl.DeviceIdType.MESH
PAIR_ROWS = 3 * HEAD_DIM
KEY_SCALE = math.log2(math.e) / math.sqrt(HEAD_DIM)
BF16 = jnp.bfloat16
F32 = jnp.float32


def nt(a, b):
    return lax.dot_general(a, b, (((1,), (1,)), ((), ())), preferred_element_type=F32)


def tn(a, b):
    return lax.dot_general(a, b, (((0,), (0,)), ((), ())), preferred_element_type=F32)


def nn(a, b):
    return jnp.dot(a, b, preferred_element_type=F32)


def layer_norm(values, norm_gain):
    average = jnp.mean(values, axis=-1, keepdims=True)
    centred = values - average
    spread = jnp.mean(centred * centred, axis=-1, keepdims=True)
    return centred * lax.rsqrt(spread + EPSILON) * norm_gain


def upsample_matrix(cols):
    taps = np.array(
        [[0.375, 0.625, 0.0], [0.125, 0.875, 0.0], [0.0, 0.875, 0.125], [0.0, 0.625, 0.375]]
    )
    pitch = cols + 2 * EDGE
    out = np.zeros((BAND, cols, 4, 3, pitch), np.float32)
    for c in range(cols):
        for t in range(4):
            for d in range(3):
                out[:, c, t, :, c + d + EDGE - 1] = taps[:, :] * taps[t, d]
    return out.reshape(BAND * cols * 4, 3 * pitch)


def value_rows(value_weight):
    rows = value_weight.T.reshape(PAIRS, 2 * HEAD_DIM, -1)
    rows = jnp.concatenate([rows, jnp.zeros_like(rows[:, :HEAD_DIM])], axis=1)
    return rows.reshape(PAIRS * PAIR_ROWS, -1)


def ones_rows():
    rows = np.zeros((PAIRS, PAIR_ROWS, BLOCK), np.float32)
    rows[:, 2 * HEAD_DIM :] = 1.0
    return rows.reshape(PAIRS * PAIR_ROWS, BLOCK)


def attend(keys, values, spread_ref):
    parts = []
    width = spread_ref.shape[1] // HEADS
    for pair in range(PAIRS):
        scores = nn(keys, spread_ref[:, pair * 2 * width : (pair + 1) * 2 * width])
        top = jnp.max(scores, axis=0, keepdims=True)
        weights = jnp.exp2((scores - top).astype(BF16))
        mix = nn(values[pair * PAIR_ROWS : (pair + 1) * PAIR_ROWS], weights)
        total = mix[2 * HEAD_DIM : 2 * HEAD_DIM + 1]
        inverse = 1.0 / total
        parts.append(mix[:HEAD_DIM, :width] * inverse[:, :width])
        parts.append(mix[HEAD_DIM : 2 * HEAD_DIM, width:] * inverse[:, width:])
    return jnp.concatenate(parts, axis=0).astype(BF16)


def query_stage(left, coarse, up_ref, wq_ref):
    up = nn(up_ref[...], coarse)
    query_in = (left.reshape(up.shape).astype(F32) + up).astype(BF16)
    return query_in, nt(wq_ref[...], query_in).astype(BF16)


def spread_queries(query_ref, spread_ref, start):
    for h in range(HEADS):
        rows = slice(h * HEAD_DIM, (h + 1) * HEAD_DIM)
        spread_ref[rows, h * BLOCK : (h + 1) * BLOCK] = query_ref[rows, pl.ds(start, BLOCK)]


def out_stage(query_in, mixed, wo_ref, gain_ref):
    product = tn(mixed, wo_ref[...])
    return layer_norm(query_in.astype(F32) + product, gain_ref[...]).astype(BF16)


def flipped(index, bit):
    return index + bit - 2 * bit * ((index // bit) % 2)


def gather_hops(n, me):
    if n != 8:
        return [(me, (me + j) % n, (me + n - j) % n, None) for j in range(1, n)]
    a, b, c = flipped(me, 1), flipped(me, 2), flipped(me, 4)
    d = flipped(b, 4)
    odd = me % 2
    relay_block = b + odd * (c - b)
    relay_target = c + odd * (b - c)
    return [
        (me, b, b, None),
        (me, c, c, None),
        (me, a, a, None),
        (relay_block, relay_target, d, (0, 1)),
        (b, a, flipped(b, 1), (0,)),
        (c, a, flipped(c, 1), (1,)),
        (d, a, flipped(d, 1), (3,)),
    ]


def gather_kernel(
    list_ref,
    count_ref,
    left_ref,
    right_ref,
    left_coarse_ref,
    right_coarse_ref,
    up_ref,
    wq_ref,
    wk_ref,
    wv_ref,
    ones_ref,
    wc_ref,
    wo_ref,
    gain_ref,
    fold_ref,
    late_ref,
    fine_ref,
    prior_ref,
    ext_ref,
    *scratch,
    n,
    row_devices,
    early,
    length,
):
    bands_ref = scratch[:early]
    (
        coarse_ref,
        edge_low_ref,
        edge_high_ref,
        rows_ref,
        query_ref,
        spread_ref,
        mix_ref,
        coarse_send,
        coarse_recv,
        edge_send,
        edge_recv,
        fine_send,
        fine_recv,
        local_sem,
    ) = scratch[early:]
    me = lax.axis_index("cols")
    row = lax.axis_index("rows")
    bands = right_ref.shape[0] // BAND
    coarse_rows, coarse_cols, feat = left_coarse_ref.shape
    hops = gather_hops(n, me)

    barrier = pltpu.get_barrier_semaphore()
    for j in range(1, n):
        pl.semaphore_signal(
            barrier, inc=1, device_id={"cols": (me + j) % n}, device_id_type=MESH
        )

    @pl.when(row > 0)
    def _():
        pl.semaphore_signal(barrier, inc=1, device_id={"rows": row - 1}, device_id_type=MESH)

    @pl.when(row < row_devices - 1)
    def _():
        pl.semaphore_signal(barrier, inc=1, device_id={"rows": row + 1}, device_id_type=MESH)

    inner = (row > 0).astype(jnp.int32) + (row < row_devices - 1).astype(jnp.int32)
    pl.semaphore_wait(barrier, n - 1 + inner)

    def coarse_copy(j):
        return pltpu.make_async_remote_copy(
            src_ref=right_coarse_ref,
            dst_ref=coarse_ref.at[me],
            send_sem=coarse_send.at[j - 1],
            recv_sem=coarse_recv.at[j - 1],
            device_id={"cols": (me + j) % n},
            device_id_type=MESH,
        )

    def place(g, block):
        if g < early:
            return bands_ref[g].at[block]
        return late_ref.at[block, pl.ds((g - early) * BAND, BAND)]

    def fine_copy(g, hop):
        block, target, _, after = hops[hop]
        if after is None:
            source = right_ref.at[pl.ds(g * BAND, BAND)]
        else:
            source = place(g, block)
        return pltpu.make_async_remote_copy(
            src_ref=source,
            dst_ref=place(g, block),
            send_sem=fine_send.at[g, hop],
            recv_sem=fine_recv.at[g, hop],
            device_id={"cols": target},
            device_id_type=MESH,
        )

    def own_copy(g):
        return pltpu.make_async_copy(
            right_ref.at[pl.ds(g * BAND, BAND)], place(g, me), local_sem.at[g]
        )

    arrived = [set() for _ in range(bands)]

    def take(g, hop):
        if hop not in arrived[g]:
            arrived[g].add(hop)
            fine_copy(g, hop).wait_recv()

    levels = []
    for hop in hops:
        levels.append(0 if hop[3] is None else 1 + max(levels[i] for i in hop[3]))
    depth = max(levels)

    def send(g, level):
        for hop in range(len(hops)):
            if levels[hop] == level:
                for needed in hops[hop][3] or ():
                    take(g, needed)
                fine_copy(g, hop).start()

    ticks = []
    for t in range(1, bands + depth):
        ticks.append(
            [(t - level, level) for level in range(depth, 0, -1) if 0 <= t - level < bands]
            + ([(t + LEAD - 1, 0)] if t + LEAD - 1 < bands else [])
        )

    def tick():
        if ticks:
            for g, level in ticks.pop(0):
                send(g, level)

    for j in range(1, n):
        coarse_copy(j).start()
    for g in range(bands):
        own_copy(g).start()
    for g in range(min(LEAD, bands)):
        send(g, 0)

    spread_ref[...] = jnp.zeros_like(spread_ref)
    coarse_ref[me] = right_coarse_ref[...]
    for j in range(1, n):
        coarse_copy(j).wait()

    wide = HEADS * coarse_cols
    diagonal = (
        lax.broadcasted_iota(jnp.int32, (feat, wide), 0) // HEAD_DIM
        == lax.broadcasted_iota(jnp.int32, (feat, wide), 1) // coarse_cols
    )

    def coarse_row(r, carry):
        right = coarse_ref[:, r].reshape(n * coarse_cols, feat)
        left = left_coarse_ref[r]
        keys = (nn(right, wk_ref[...]) * KEY_SCALE).astype(BF16)
        values = nt(wc_ref[...], right).astype(BF16)
        queries = nt(wq_ref[...], jnp.concatenate([left] * HEADS, axis=0))
        queries = jnp.where(diagonal, queries, 0.0).astype(BF16)
        scores = nn(keys, queries)
        top = jnp.max(scores, axis=0, keepdims=True)
        weights = jnp.exp2((scores - top).astype(BF16))
        total = jnp.sum(weights.astype(F32), axis=0, keepdims=True)
        mixed = nn(values, weights) * (1.0 / total)
        mixed = jnp.where(diagonal, mixed, 0.0).astype(BF16)
        folded = nt(fold_ref[...], mixed).astype(BF16)
        out = left.astype(F32) + nn(folded, wo_ref[...])
        out = layer_norm(out, gain_ref[...]).astype(BF16)
        rows_ref[r + 1] = out
        prior_ref[r] = out
        return carry

    lax.fori_loop(0, coarse_rows // 2, coarse_row, 0)
    tick()
    lax.fori_loop(coarse_rows // 2, coarse_rows, coarse_row, 0)

    def row_copy(up):
        return pltpu.make_async_remote_copy(
            src_ref=prior_ref.at[0 if up else coarse_rows - 1],
            dst_ref=rows_ref.at[coarse_rows + 1 if up else 0],
            send_sem=edge_send.at[0 if up else 1],
            recv_sem=edge_recv.at[0 if up else 1],
            device_id={"rows": row - 1 if up else row + 1},
            device_id_type=MESH,
        )

    def col_copy(left):
        return pltpu.make_async_remote_copy(
            src_ref=rows_ref.at[:, pl.ds(0 if left else coarse_cols - EDGE, EDGE)],
            dst_ref=edge_high_ref if left else edge_low_ref,
            send_sem=edge_send.at[2 if left else 3],
            recv_sem=edge_recv.at[2 if left else 3],
            device_id={"cols": me - 1 if left else me + 1},
            device_id_type=MESH,
        )

    has = (row > 0, row < row_devices - 1, me > 0, me < n - 1)

    @pl.when(has[0])
    def _():
        row_copy(True).start()

    @pl.when(has[1])
    def _():
        row_copy(False).start()

    @pl.when(has[0])
    def _():
        row_copy(False).wait_recv()
        row_copy(True).wait_send()

    @pl.when(jnp.logical_not(has[0]))
    def _():
        rows_ref[0] = rows_ref[1]

    @pl.when(has[1])
    def _():
        row_copy(True).wait_recv()
        row_copy(False).wait_send()

    @pl.when(jnp.logical_not(has[1]))
    def _():
        rows_ref[coarse_rows + 1] = rows_ref[coarse_rows]

    @pl.when(has[2])
    def _():
        col_copy(True).start()

    @pl.when(has[3])
    def _():
        col_copy(False).start()

    tick()

    @pl.when(has[2])
    def _():
        col_copy(False).wait_recv()
        col_copy(True).wait_send()

    @pl.when(jnp.logical_not(has[2]))
    def _():
        edge_low_ref[...] = jnp.broadcast_to(rows_ref[:, 0:1], edge_low_ref.shape)

    @pl.when(has[3])
    def _():
        col_copy(True).wait_recv()
        col_copy(False).wait_send()

    @pl.when(jnp.logical_not(has[3]))
    def _():
        edge_high_ref[...] = jnp.broadcast_to(
            rows_ref[:, coarse_cols - 1 : coarse_cols], edge_high_ref.shape
        )

    ext_ref[:, :EDGE] = edge_low_ref[...]
    ext_ref[:, EDGE : EDGE + coarse_cols] = rows_ref[...]
    ext_ref[:, EDGE + coarse_cols :] = edge_high_ref[...]

    for g in range(early):
        if g > 0:
            tick()
        own_copy(g).wait()
        for hop in range(len(hops)):
            take(g, hop)
        coarse = jnp.concatenate([ext_ref[g + i] for i in range(3)], axis=0)
        query_in, queries = query_stage(left_ref[g * BAND : (g + 1) * BAND], coarse, up_ref, wq_ref)
        query_ref[...] = queries
        used = count_ref[g]
        picks = [
            jnp.where(k < used, list_ref[g * length + k], list_ref[g * length])
            for k in range(length)
        ]
        flags = [jnp.where(k < used, 1.0, 0.0) for k in range(length)]

        def fine_row(r, carry, g=g, picks=picks, flags=flags):
            keys, values = [], []
            for k in range(length):
                block = bands_ref[g][picks[k], r]
                keys.append((nn(block, wk_ref[...]) * KEY_SCALE).astype(BF16))
                values.append(((nt(wv_ref[...], block) + ones_ref[...]) * flags[k]).astype(BF16))
            keys = jnp.concatenate(keys, axis=0)
            values = jnp.concatenate(values, axis=1)
            start = pl.multiple_of(r * BLOCK, BLOCK)
            spread_queries(query_ref, spread_ref, start)
            mix_ref[:, pl.ds(start, BLOCK)] = attend(keys, values, spread_ref)
            return carry

        lax.fori_loop(0, BAND // 2, fine_row, 0)
        tick()
        lax.fori_loop(BAND // 2, BAND, fine_row, 0)
        out = out_stage(query_in, mix_ref[...], wo_ref, gain_ref)
        fine_ref[g * BAND : (g + 1) * BAND] = out.reshape(BAND, BLOCK, feat)

    while ticks:
        tick()
    for g in range(bands):
        if g >= early:
            own_copy(g).wait()
        for hop in range(len(hops)):
            take(g, hop)
            fine_copy(g, hop).wait_send()


def gather_stage(mesh_rows, n, left_fine, right_fine, left_coarse, right_coarse, lists, counts, w):
    rows, cols, feat = left_fine.shape
    bands = rows // BAND
    early = min(EARLY, bands - 1)
    coarse_rows, coarse_cols, _ = left_coarse.shape
    fold = np.tile(np.eye(coarse_cols, dtype=np.float32), (1, HEADS))
    hop_count = len(gather_hops(n, 0))
    vmem = pl.BlockSpec(memory_space=pltpu.VMEM)
    smem = pl.BlockSpec(memory_space=pltpu.SMEM)
    return pl.pallas_call(
        functools.partial(
            gather_kernel, n=n, row_devices=mesh_rows, early=early, length=lists.shape[1]
        ),
        out_shape=(
            jax.ShapeDtypeStruct((n, (bands - early) * BAND, cols, feat), BF16),
            jax.ShapeDtypeStruct(left_fine.shape, BF16),
            jax.ShapeDtypeStruct(left_coarse.shape, BF16),
            jax.ShapeDtypeStruct((coarse_rows + 2, coarse_cols + 2 * EDGE, feat), BF16),
        ),
        in_specs=[smem, smem] + [vmem] * 13,
        out_specs=(pl.BlockSpec(memory_space=pl.ANY), vmem, vmem, vmem),
        scratch_shapes=[pltpu.VMEM((n, BAND, cols, feat), BF16) for _ in range(early)]
        + [
            pltpu.VMEM((n,) + right_coarse.shape, BF16),
            pltpu.VMEM((coarse_rows + 2, EDGE, feat), BF16),
            pltpu.VMEM((coarse_rows + 2, EDGE, feat), BF16),
            pltpu.VMEM((coarse_rows + 2, coarse_cols, feat), BF16),
            pltpu.VMEM((feat, BAND * BLOCK), BF16),
            pltpu.VMEM((feat, HEADS * BLOCK), BF16),
            pltpu.VMEM((feat, BAND * BLOCK), BF16),
            pltpu.SemaphoreType.DMA((n - 1,)),
            pltpu.SemaphoreType.DMA((n - 1,)),
            pltpu.SemaphoreType.DMA((4,)),
            pltpu.SemaphoreType.DMA((4,)),
            pltpu.SemaphoreType.DMA((bands, hop_count)),
            pltpu.SemaphoreType.DMA((bands, hop_count)),
            pltpu.SemaphoreType.DMA((bands,)),
        ],
        compiler_params=pltpu.CompilerParams(collective_id=0, has_side_effects=True),
        name="gather_stage",
    )(
        lists.reshape(-1),
        counts,
        left_fine,
        right_fine,
        left_coarse,
        right_coarse,
        w["up"],
        w["wq"],
        w["wk"],
        w["vrows"],
        w["ones"],
        w["wc"],
        w["wo"],
        w["gain"],
        jnp.asarray(fold, BF16),
    )


def fine_kernel(
    list_ref,
    count_ref,
    left_ref,
    ext_ref,
    up_ref,
    wq_ref,
    wk_ref,
    wv_ref,
    ones_ref,
    wo_ref,
    gain_ref,
    done_ref,
    *refs,
    early,
):
    del done_ref
    list_length = len(refs) - 4
    cand_refs = refs[:list_length]
    out_ref, query_ref, spread_ref, mix_ref = refs[list_length:]
    band = pl.program_id(0) + early
    feat = wq_ref.shape[0]

    @pl.when(pl.program_id(0) == 0)
    def _():
        spread_ref[...] = jnp.zeros_like(spread_ref)

    coarse = jnp.concatenate([ext_ref[band + i] for i in range(3)], axis=0)
    query_in, queries = query_stage(left_ref[...], coarse, up_ref, wq_ref)
    query_ref[...] = queries

    for used in range(1, list_length + 1):

        @pl.when(count_ref[band] == used)
        def _():
            def row(r, carry):
                keys, values = [], []
                for k in range(used):
                    block = cand_refs[k][0, r]
                    keys.append((nn(block, wk_ref[...]) * KEY_SCALE).astype(BF16))
                    values.append((nt(wv_ref[...], block) + ones_ref[...]).astype(BF16))
                keys = jnp.concatenate(keys, axis=0)
                values = jnp.concatenate(values, axis=1)
                start = pl.multiple_of(r * BLOCK, BLOCK)
                spread_queries(query_ref, spread_ref, start)
                mix_ref[:, pl.ds(start, BLOCK)] = attend(keys, values, spread_ref)
                return carry

            lax.fori_loop(0, BAND, row, 0)

    out_ref[...] = out_stage(query_in, mix_ref[...], wo_ref, gain_ref).reshape(out_ref.shape)


def fine_stage(left_fine, gathered, done, ext, lists, counts, w):
    rows, cols, feat = left_fine.shape
    bands = rows // BAND
    early = bands - gathered.shape[1] // BAND
    length = lists.shape[1]

    def whole(shape):
        return pl.BlockSpec(shape, lambda g, c, n: (0,) * len(shape))

    def picked(k):
        return pl.BlockSpec(
            (1, BAND, cols, feat), lambda g, c, n: (c[(g + early) * length + k], g, 0, 0)
        )

    def banded():
        return pl.BlockSpec((BAND, cols, feat), lambda g, c, n: (g + early, 0, 0))

    names = ("up", "wq", "wk", "vrows", "ones", "wo", "gain")
    return pl.pallas_call(
        functools.partial(fine_kernel, early=early),
        grid_spec=pltpu.PrefetchScalarGridSpec(
            num_scalar_prefetch=2,
            grid=(bands - early,),
            in_specs=[banded(), whole(ext.shape)]
            + [whole(w[name].shape) for name in names]
            + [pl.BlockSpec(memory_space=pl.ANY)]
            + [picked(k) for k in range(length)],
            out_specs=banded(),
            scratch_shapes=[
                pltpu.VMEM((feat, BAND * BLOCK), BF16),
                pltpu.VMEM((feat, HEADS * BLOCK), BF16),
                pltpu.VMEM((feat, BAND * BLOCK), BF16),
            ],
        ),
        out_shape=jax.ShapeDtypeStruct(left_fine.shape, BF16),
        input_output_aliases={4 + len(names): 0},
        name="fine_stage",
    )(
        lists.reshape(-1),
        counts,
        left_fine,
        ext,
        *[w[name] for name in names],
        done,
        *([gathered] * length),
    )


def body(
    left_fine,
    right_fine,
    left_coarse,
    right_coarse,
    candidates,
    counts,
    query_weight,
    key_weight,
    value_weight,
    out_weight,
    norm_gain,
):
    me = lax.axis_index("cols")
    lists = lax.dynamic_index_in_dim(candidates, me, 0, keepdims=False)
    own_counts = lax.dynamic_index_in_dim(counts, me, 0, keepdims=False)
    w = {
        "up": jnp.asarray(upsample_matrix(left_coarse.shape[1]), BF16),
        "wq": query_weight.T,
        "wk": key_weight,
        "vrows": value_rows(value_weight),
        "wc": value_weight.T,
        "ones": jnp.asarray(ones_rows(), F32),
        "wo": out_weight,
        "gain": norm_gain.reshape(1, -1),
    }
    gathered, done, coarse_prior, ext = gather_stage(
        lax.axis_size("rows"),
        lax.axis_size("cols"),
        left_fine,
        right_fine,
        left_coarse,
        right_coarse,
        lists,
        own_counts,
        w,
    )
    fine_features = fine_stage(left_fine, gathered, done, ext, lists, own_counts, w)
    return (fine_features, coarse_prior)


def solution(mesh):
    return jax.shard_map(
        body,
        mesh=mesh,
        in_specs=(
            P("rows", "cols", None),
            P("rows", "cols", None),
            P("rows", "cols", None),
            P("rows", "cols", None),
            P(None, "rows", None),
            P(None, "rows"),
            P(),
            P(),
            P(),
            P(),
            P(),
        ),
        out_specs=(P("rows", "cols", None), P("rows", "cols", None)),
        check_vma=False,
    )
```

```python
import functools
import math

import jax
import jax.numpy as jnp
import numpy as np
from jax import lax
from jax.experimental import pallas as pl
from jax.experimental.pallas import tpu as pltpu
from jax.sharding import PartitionSpec as P

HEADS = 8
HEAD_DIM = 16
BLOCK = 128
BAND = 4
EPSILON = 1e-05
PAIRS = HEADS // 2
EDGE = 16
EARLY = 2
LEAD = 3
MESH = pl.DeviceIdType.MESH
KEY_SCALE = math.log2(math.e) / math.sqrt(HEAD_DIM)
BF16 = jnp.bfloat16
F32 = jnp.float32


def nt(a, b):
    return lax.dot_general(a, b, (((1,), (1,)), ((), ())), preferred_element_type=F32)


def tn(a, b):
    return lax.dot_general(a, b, (((0,), (0,)), ((), ())), preferred_element_type=F32)


def nn(a, b):
    return jnp.dot(a, b, preferred_element_type=F32)


def layer_norm(values, norm_gain):
    average = jnp.mean(values, axis=-1, keepdims=True)
    centred = values - average
    spread = jnp.mean(centred * centred, axis=-1, keepdims=True)
    return centred * lax.rsqrt(spread + EPSILON) * norm_gain


def upsample_matrix(cols):
    taps = np.array(
        [[0.375, 0.625, 0.0], [0.125, 0.875, 0.0], [0.0, 0.875, 0.125], [0.0, 0.625, 0.375]]
    )
    pitch = cols + 2 * EDGE
    out = np.zeros((BAND, cols, 4, 3, pitch), np.float32)
    for c in range(cols):
        for t in range(4):
            for d in range(3):
                out[:, c, t, :, c + d + EDGE - 1] = taps[:, :] * taps[t, d]
    return out.reshape(BAND * cols * 4, 3 * pitch)


def project_blocks(blocks, wkv_ref):
    feat = blocks[0].shape[1]
    keys, values = [], []
    for block in blocks:
        both = nn(block, wkv_ref[...])
        keys.append((both[:, :feat] * KEY_SCALE).astype(BF16))
        values.append(both[:, feat:].astype(BF16).T)
    return jnp.concatenate(keys, axis=0), jnp.concatenate(values, axis=1)


def attend(keys, values, ones, spread_ref):
    parts = []
    width = spread_ref.shape[1] // HEADS

    def score(pair):
        return nn(keys, spread_ref[:, pair * 2 * width : (pair + 1) * 2 * width])

    ahead = score(0)
    for pair in range(PAIRS):
        scores = ahead
        if pair + 1 < PAIRS:
            ahead = score(pair + 1)
        top = jnp.max(scores, axis=0, keepdims=True)
        weights = jnp.exp2((scores - top).astype(BF16))
        rows = values[pair * 2 * HEAD_DIM : (pair + 1) * 2 * HEAD_DIM]
        mix = nn(jnp.concatenate([rows, ones], axis=0), weights)
        inverse = 1.0 / mix[2 * HEAD_DIM : 2 * HEAD_DIM + 1]
        parts.append(mix[:HEAD_DIM, :width] * inverse[:, :width])
        parts.append(mix[HEAD_DIM : 2 * HEAD_DIM, width:] * inverse[:, width:])
    return jnp.concatenate(parts, axis=0).astype(BF16)


def query_stage(left, coarse, up_ref, wq_ref):
    up = nn(up_ref[...], coarse)
    query_in = (left.reshape(up.shape).astype(F32) + up).astype(BF16)
    return query_in, nt(wq_ref[...], query_in).astype(BF16)


def spread_queries(query_ref, spread_ref, start):
    for h in range(HEADS):
        rows = slice(h * HEAD_DIM, (h + 1) * HEAD_DIM)
        spread_ref[rows, h * BLOCK : (h + 1) * BLOCK] = query_ref[rows, pl.ds(start, BLOCK)]


def out_stage(query_in, mixed, wo_ref, gain_ref):
    product = tn(mixed, wo_ref[...])
    return layer_norm(query_in.astype(F32) + product, gain_ref[...]).astype(BF16)


def flipped(index, bit):
    return index + bit - 2 * bit * ((index // bit) % 2)


def gather_hops(n, me):
    if n != 8:
        return [(me, (me + j) % n, (me + n - j) % n, None) for j in range(1, n)]
    a, b, c = flipped(me, 1), flipped(me, 2), flipped(me, 4)
    d = flipped(b, 4)
    odd = me % 2
    relay_block = b + odd * (c - b)
    relay_target = c + odd * (b - c)
    return [
        (me, b, b, None),
        (me, c, c, None),
        (me, a, a, None),
        (relay_block, relay_target, d, (0, 1)),
        (b, a, flipped(b, 1), (0,)),
        (c, a, flipped(c, 1), (1,)),
        (d, a, flipped(d, 1), (3,)),
    ]


def gather_kernel(
    list_ref,
    count_ref,
    left_ref,
    right_ref,
    left_coarse_ref,
    right_coarse_ref,
    up_ref,
    wq_ref,
    wkv_ref,
    wc_ref,
    wo_ref,
    gain_ref,
    fold_ref,
    late_ref,
    fine_ref,
    prior_ref,
    ext_ref,
    *scratch,
    n,
    row_devices,
    early,
    length,
):
    bands_ref = scratch[:early]
    (
        coarse_ref,
        edge_low_ref,
        edge_high_ref,
        rows_ref,
        query_ref,
        spread_ref,
        mix_ref,
        coarse_send,
        coarse_recv,
        edge_send,
        edge_recv,
        fine_send,
        fine_recv,
        local_sem,
    ) = scratch[early:]
    me = lax.axis_index("cols")
    row = lax.axis_index("rows")
    bands = right_ref.shape[0] // BAND
    coarse_rows, coarse_cols, feat = left_coarse_ref.shape
    hops = gather_hops(n, me)

    barrier = pltpu.get_barrier_semaphore()
    for j in range(1, n):
        pl.semaphore_signal(
            barrier, inc=1, device_id={"cols": (me + j) % n}, device_id_type=MESH
        )

    @pl.when(row > 0)
    def _():
        pl.semaphore_signal(barrier, inc=1, device_id={"rows": row - 1}, device_id_type=MESH)

    @pl.when(row < row_devices - 1)
    def _():
        pl.semaphore_signal(barrier, inc=1, device_id={"rows": row + 1}, device_id_type=MESH)

    inner = (row > 0).astype(jnp.int32) + (row < row_devices - 1).astype(jnp.int32)
    pl.semaphore_wait(barrier, n - 1 + inner)

    def coarse_copy(j):
        return pltpu.make_async_remote_copy(
            src_ref=right_coarse_ref,
            dst_ref=coarse_ref.at[me],
            send_sem=coarse_send.at[j - 1],
            recv_sem=coarse_recv.at[j - 1],
            device_id={"cols": (me + j) % n},
            device_id_type=MESH,
        )

    def place(g, block):
        if g < early:
            return bands_ref[g].at[block]
        return late_ref.at[block, pl.ds((g - early) * BAND, BAND)]

    def fine_copy(g, hop):
        block, target, _, after = hops[hop]
        if after is None:
            source = right_ref.at[pl.ds(g * BAND, BAND)]
        else:
            source = place(g, block)
        return pltpu.make_async_remote_copy(
            src_ref=source,
            dst_ref=place(g, block),
            send_sem=fine_send.at[g, hop],
            recv_sem=fine_recv.at[g, hop],
            device_id={"cols": target},
            device_id_type=MESH,
        )

    def own_copy(g):
        return pltpu.make_async_copy(
            right_ref.at[pl.ds(g * BAND, BAND)], place(g, me), local_sem.at[g]
        )

    arrived = [set() for _ in range(bands)]

    def take(g, hop):
        if hop not in arrived[g]:
            arrived[g].add(hop)
            fine_copy(g, hop).wait_recv()

    levels = []
    for hop in hops:
        levels.append(0 if hop[3] is None else 1 + max(levels[i] for i in hop[3]))
    depth = max(levels)

    def send(g, level):
        for hop in range(len(hops)):
            if levels[hop] == level:
                for needed in hops[hop][3] or ():
                    take(g, needed)
                fine_copy(g, hop).start()

    ticks = []
    for t in range(1, bands + depth):
        ticks.append(
            [(t - level, level) for level in range(depth, 0, -1) if 0 <= t - level < bands]
            + ([(t + LEAD - 1, 0)] if t + LEAD - 1 < bands else [])
        )

    def tick():
        if ticks:
            for g, level in ticks.pop(0):
                send(g, level)

    for j in range(1, n):
        coarse_copy(j).start()
    for g in range(bands):
        own_copy(g).start()
    for g in range(min(LEAD, bands)):
        send(g, 0)

    spread_ref[...] = jnp.zeros_like(spread_ref)
    coarse_ref[me] = right_coarse_ref[...]
    for j in range(1, n):
        coarse_copy(j).wait()

    wide = HEADS * coarse_cols
    diagonal = (
        lax.broadcasted_iota(jnp.int32, (feat, wide), 0) // HEAD_DIM
        == lax.broadcasted_iota(jnp.int32, (feat, wide), 1) // coarse_cols
    )

    def coarse_row(r, carry):
        right = coarse_ref[:, r].reshape(n * coarse_cols, feat)
        left = left_coarse_ref[r]
        keys = (nn(right, wkv_ref[:, :feat]) * KEY_SCALE).astype(BF16)
        values = nt(wc_ref[...], right).astype(BF16)
        queries = nt(wq_ref[...], jnp.concatenate([left] * HEADS, axis=0))
        queries = jnp.where(diagonal, queries, 0.0).astype(BF16)
        scores = nn(keys, queries)
        top = jnp.max(scores, axis=0, keepdims=True)
        weights = jnp.exp2((scores - top).astype(BF16))
        total = jnp.sum(weights.astype(F32), axis=0, keepdims=True)
        mixed = nn(values, weights) * (1.0 / total)
        mixed = jnp.where(diagonal, mixed, 0.0).astype(BF16)
        folded = nt(fold_ref[...], mixed).astype(BF16)
        out = left.astype(F32) + nn(folded, wo_ref[...])
        out = layer_norm(out, gain_ref[...]).astype(BF16)
        rows_ref[r + 1] = out
        prior_ref[r] = out
        return carry

    lax.fori_loop(0, coarse_rows // 2, coarse_row, 0)
    tick()
    lax.fori_loop(coarse_rows // 2, coarse_rows, coarse_row, 0)

    def row_copy(up):
        return pltpu.make_async_remote_copy(
            src_ref=prior_ref.at[0 if up else coarse_rows - 1],
            dst_ref=rows_ref.at[coarse_rows + 1 if up else 0],
            send_sem=edge_send.at[0 if up else 1],
            recv_sem=edge_recv.at[0 if up else 1],
            device_id={"rows": row - 1 if up else row + 1},
            device_id_type=MESH,
        )

    def col_copy(left):
        return pltpu.make_async_remote_copy(
            src_ref=rows_ref.at[:, pl.ds(0 if left else coarse_cols - EDGE, EDGE)],
            dst_ref=edge_high_ref if left else edge_low_ref,
            send_sem=edge_send.at[2 if left else 3],
            recv_sem=edge_recv.at[2 if left else 3],
            device_id={"cols": me - 1 if left else me + 1},
            device_id_type=MESH,
        )

    has = (row > 0, row < row_devices - 1, me > 0, me < n - 1)

    @pl.when(has[0])
    def _():
        row_copy(True).start()

    @pl.when(has[1])
    def _():
        row_copy(False).start()

    @pl.when(has[0])
    def _():
        row_copy(False).wait_recv()
        row_copy(True).wait_send()

    @pl.when(jnp.logical_not(has[0]))
    def _():
        rows_ref[0] = rows_ref[1]

    @pl.when(has[1])
    def _():
        row_copy(True).wait_recv()
        row_copy(False).wait_send()

    @pl.when(jnp.logical_not(has[1]))
    def _():
        rows_ref[coarse_rows + 1] = rows_ref[coarse_rows]

    @pl.when(has[2])
    def _():
        col_copy(True).start()

    @pl.when(has[3])
    def _():
        col_copy(False).start()

    tick()

    @pl.when(has[2])
    def _():
        col_copy(False).wait_recv()
        col_copy(True).wait_send()

    @pl.when(jnp.logical_not(has[2]))
    def _():
        edge_low_ref[...] = jnp.broadcast_to(rows_ref[:, 0:1], edge_low_ref.shape)

    @pl.when(has[3])
    def _():
        col_copy(True).wait_recv()
        col_copy(False).wait_send()

    @pl.when(jnp.logical_not(has[3]))
    def _():
        edge_high_ref[...] = jnp.broadcast_to(
            rows_ref[:, coarse_cols - 1 : coarse_cols], edge_high_ref.shape
        )

    ext_ref[:, :EDGE] = edge_low_ref[...]
    ext_ref[:, EDGE : EDGE + coarse_cols] = rows_ref[...]
    ext_ref[:, EDGE + coarse_cols :] = edge_high_ref[...]

    for g in range(early):
        if g > 0:
            tick()
        own_copy(g).wait()
        for hop in range(len(hops)):
            take(g, hop)
        coarse = jnp.concatenate([ext_ref[g + i] for i in range(3)], axis=0)
        query_in, queries = query_stage(left_ref[g * BAND : (g + 1) * BAND], coarse, up_ref, wq_ref)
        query_ref[...] = queries
        used = count_ref[g]
        picks = [
            jnp.where(k < used, list_ref[g * length + k], list_ref[g * length])
            for k in range(length)
        ]
        lanes = lax.broadcasted_iota(jnp.int32, (1, length * BLOCK), 1)
        live = jnp.where(lanes < used * BLOCK, 1.0, 0.0).astype(BF16)

        def fine_row(r, carry, g=g, picks=picks, live=live):
            keys, values = project_blocks(
                [bands_ref[g][picks[k], r] for k in range(length)], wkv_ref
            )
            values = values * live
            ones = jnp.broadcast_to(live, (HEAD_DIM, live.shape[1]))
            start = pl.multiple_of(r * BLOCK, BLOCK)
            spread_queries(query_ref, spread_ref, start)
            mix_ref[:, pl.ds(start, BLOCK)] = attend(keys, values, ones, spread_ref)
            return carry

        lax.fori_loop(0, BAND // 2, fine_row, 0)
        tick()
        lax.fori_loop(BAND // 2, BAND, fine_row, 0)
        out = out_stage(query_in, mix_ref[...], wo_ref, gain_ref)
        fine_ref[g * BAND : (g + 1) * BAND] = out.reshape(BAND, BLOCK, feat)

    while ticks:
        tick()
    for g in range(bands):
        if g >= early:
            own_copy(g).wait()
        for hop in range(len(hops)):
            take(g, hop)
            fine_copy(g, hop).wait_send()


def gather_stage(mesh_rows, n, left_fine, right_fine, left_coarse, right_coarse, lists, counts, w):
    rows, cols, feat = left_fine.shape
    bands = rows // BAND
    early = min(EARLY, bands - 1)
    coarse_rows, coarse_cols, _ = left_coarse.shape
    fold = np.tile(np.eye(coarse_cols, dtype=np.float32), (1, HEADS))
    hop_count = len(gather_hops(n, 0))
    vmem = pl.BlockSpec(memory_space=pltpu.VMEM)
    smem = pl.BlockSpec(memory_space=pltpu.SMEM)
    return pl.pallas_call(
        functools.partial(
            gather_kernel, n=n, row_devices=mesh_rows, early=early, length=lists.shape[1]
        ),
        out_shape=(
            jax.ShapeDtypeStruct((n, (bands - early) * BAND, cols, feat), BF16),
            jax.ShapeDtypeStruct(left_fine.shape, BF16),
            jax.ShapeDtypeStruct(left_coarse.shape, BF16),
            jax.ShapeDtypeStruct((coarse_rows + 2, coarse_cols + 2 * EDGE, feat), BF16),
        ),
        in_specs=[smem, smem] + [vmem] * 11,
        out_specs=(pl.BlockSpec(memory_space=pl.ANY), vmem, vmem, vmem),
        scratch_shapes=[pltpu.VMEM((n, BAND, cols, feat), BF16) for _ in range(early)]
        + [
            pltpu.VMEM((n,) + right_coarse.shape, BF16),
            pltpu.VMEM((coarse_rows + 2, EDGE, feat), BF16),
            pltpu.VMEM((coarse_rows + 2, EDGE, feat), BF16),
            pltpu.VMEM((coarse_rows + 2, coarse_cols, feat), BF16),
            pltpu.VMEM((feat, BAND * BLOCK), BF16),
            pltpu.VMEM((feat, HEADS * BLOCK), BF16),
            pltpu.VMEM((feat, BAND * BLOCK), BF16),
            pltpu.SemaphoreType.DMA((n - 1,)),
            pltpu.SemaphoreType.DMA((n - 1,)),
            pltpu.SemaphoreType.DMA((4,)),
            pltpu.SemaphoreType.DMA((4,)),
            pltpu.SemaphoreType.DMA((bands, hop_count)),
            pltpu.SemaphoreType.DMA((bands, hop_count)),
            pltpu.SemaphoreType.DMA((bands,)),
        ],
        compiler_params=pltpu.CompilerParams(collective_id=0, has_side_effects=True),
        name="gather_stage",
    )(
        lists.reshape(-1),
        counts,
        left_fine,
        right_fine,
        left_coarse,
        right_coarse,
        w["up"],
        w["wq"],
        w["wkv"],
        w["wc"],
        w["wo"],
        w["gain"],
        jnp.asarray(fold, BF16),
    )


def fine_kernel(
    list_ref,
    count_ref,
    left_ref,
    ext_ref,
    up_ref,
    wq_ref,
    wkv_ref,
    wo_ref,
    gain_ref,
    done_ref,
    *refs,
    early,
):
    del done_ref
    list_length = len(refs) - 4
    cand_refs = refs[:list_length]
    out_ref, query_ref, spread_ref, mix_ref = refs[list_length:]
    band = pl.program_id(0) + early
    feat = wq_ref.shape[0]

    @pl.when(pl.program_id(0) == 0)
    def _():
        spread_ref[...] = jnp.zeros_like(spread_ref)

    coarse = jnp.concatenate([ext_ref[band + i] for i in range(3)], axis=0)
    query_in, queries = query_stage(left_ref[...], coarse, up_ref, wq_ref)
    query_ref[...] = queries

    for used in range(1, list_length + 1):

        @pl.when(count_ref[band] == used)
        def _():
            def row(r, carry):
                keys, values = project_blocks(
                    [cand_refs[k][0, r] for k in range(used)], wkv_ref
                )
                ones = jnp.ones((HEAD_DIM, used * BLOCK), BF16)
                start = pl.multiple_of(r * BLOCK, BLOCK)
                spread_queries(query_ref, spread_ref, start)
                mix_ref[:, pl.ds(start, BLOCK)] = attend(keys, values, ones, spread_ref)
                return carry

            lax.fori_loop(0, BAND, row, 0)

    out_ref[...] = out_stage(query_in, mix_ref[...], wo_ref, gain_ref).reshape(out_ref.shape)


def fine_stage(left_fine, gathered, done, ext, lists, counts, w):
    rows, cols, feat = left_fine.shape
    bands = rows // BAND
    early = bands - gathered.shape[1] // BAND
    length = lists.shape[1]

    def whole(shape):
        return pl.BlockSpec(shape, lambda g, c, n: (0,) * len(shape))

    def picked(k):
        return pl.BlockSpec(
            (1, BAND, cols, feat), lambda g, c, n: (c[(g + early) * length + k], g, 0, 0)
        )

    def banded():
        return pl.BlockSpec((BAND, cols, feat), lambda g, c, n: (g + early, 0, 0))

    names = ("up", "wq", "wkv", "wo", "gain")
    return pl.pallas_call(
        functools.partial(fine_kernel, early=early),
        grid_spec=pltpu.PrefetchScalarGridSpec(
            num_scalar_prefetch=2,
            grid=(bands - early,),
            in_specs=[banded(), whole(ext.shape)]
            + [whole(w[name].shape) for name in names]
            + [pl.BlockSpec(memory_space=pl.ANY)]
            + [picked(k) for k in range(length)],
            out_specs=banded(),
            scratch_shapes=[
                pltpu.VMEM((feat, BAND * BLOCK), BF16),
                pltpu.VMEM((feat, HEADS * BLOCK), BF16),
                pltpu.VMEM((feat, BAND * BLOCK), BF16),
            ],
        ),
        out_shape=jax.ShapeDtypeStruct(left_fine.shape, BF16),
        input_output_aliases={4 + len(names): 0},
        name="fine_stage",
    )(
        lists.reshape(-1),
        counts,
        left_fine,
        ext,
        *[w[name] for name in names],
        done,
        *([gathered] * length),
    )


def body(
    left_fine,
    right_fine,
    left_coarse,
    right_coarse,
    candidates,
    counts,
    query_weight,
    key_weight,
    value_weight,
    out_weight,
    norm_gain,
):
    me = lax.axis_index("cols")
    lists = lax.dynamic_index_in_dim(candidates, me, 0, keepdims=False)
    own_counts = lax.dynamic_index_in_dim(counts, me, 0, keepdims=False)
    w = {
        "up": jnp.asarray(upsample_matrix(left_coarse.shape[1]), BF16),
        "wq": query_weight.T,
        "wkv": jnp.concatenate([key_weight, value_weight], axis=1),
        "wc": value_weight.T,
        "wo": out_weight,
        "gain": norm_gain.reshape(1, -1),
    }
    gathered, done, coarse_prior, ext = gather_stage(
        lax.axis_size("rows"),
        lax.axis_size("cols"),
        left_fine,
        right_fine,
        left_coarse,
        right_coarse,
        lists,
        own_counts,
        w,
    )
    fine_features = fine_stage(left_fine, gathered, done, ext, lists, own_counts, w)
    return (fine_features, coarse_prior)


def solution(mesh):
    return jax.shard_map(
        body,
        mesh=mesh,
        in_specs=(
            P("rows", "cols", None),
            P("rows", "cols", None),
            P("rows", "cols", None),
            P("rows", "cols", None),
            P(None, "rows", None),
            P(None, "rows"),
            P(),
            P(),
            P(),
            P(),
            P(),
        ),
        out_specs=(P("rows", "cols", None), P("rows", "cols", None)),
        check_vma=False,
    )
```

```python
import functools
import math

import jax
import jax.numpy as jnp
import numpy as np
from jax import lax
from jax.experimental import pallas as pl
from jax.experimental.pallas import tpu as pltpu
from jax.sharding import PartitionSpec as P

HEADS = 8
HEAD_DIM = 16
BLOCK = 128
BAND = 4
EPSILON = 1e-05
PAIRS = HEADS // 2
EDGE = 16
EARLY = 3
LEAD = 5
MESH = pl.DeviceIdType.MESH
KEY_SCALE = math.log2(math.e) / math.sqrt(HEAD_DIM)
BF16 = jnp.bfloat16
F32 = jnp.float32


def nt(a, b):
    return lax.dot_general(a, b, (((1,), (1,)), ((), ())), preferred_element_type=F32)


def tn(a, b):
    return lax.dot_general(a, b, (((0,), (0,)), ((), ())), preferred_element_type=F32)


def nn(a, b):
    return jnp.dot(a, b, preferred_element_type=F32)


def layer_norm(values, norm_gain):
    average = jnp.mean(values, axis=-1, keepdims=True)
    centred = values - average
    spread = jnp.mean(centred * centred, axis=-1, keepdims=True)
    return centred * lax.rsqrt(spread + EPSILON) * norm_gain


def upsample_matrix(cols):
    taps = np.array(
        [[0.375, 0.625, 0.0], [0.125, 0.875, 0.0], [0.0, 0.875, 0.125], [0.0, 0.625, 0.375]]
    )
    pitch = cols + 2 * EDGE
    out = np.zeros((BAND, cols, 4, 3, pitch), np.float32)
    for c in range(cols):
        for t in range(4):
            for d in range(3):
                out[:, c, t, :, c + d + EDGE - 1] = taps[:, :] * taps[t, d]
    return out.reshape(BAND * cols * 4, 3 * pitch)


def project_blocks(blocks, wkv_ref):
    feat = blocks[0].shape[1]
    keys, values = [], []
    for block in blocks:
        both = nn(block, wkv_ref[...])
        keys.append((both[:, :feat] * KEY_SCALE).astype(BF16))
        values.append(both[:, feat:].astype(BF16).T)
    return jnp.concatenate(keys, axis=0), jnp.concatenate(values, axis=1)


def attend(keys, values, ones, spread_ref):
    parts = []
    width = spread_ref.shape[1] // HEADS

    def score(pair):
        return nn(keys, spread_ref[:, pair * 2 * width : (pair + 1) * 2 * width])

    ahead = score(0)
    for pair in range(PAIRS):
        scores = ahead
        if pair + 1 < PAIRS:
            ahead = score(pair + 1)
        top = jnp.max(scores, axis=0, keepdims=True)
        weights = jnp.exp2((scores - top).astype(BF16))
        rows = values[pair * 2 * HEAD_DIM : (pair + 1) * 2 * HEAD_DIM]
        mix = nn(jnp.concatenate([rows, ones], axis=0), weights)
        inverse = 1.0 / mix[2 * HEAD_DIM : 2 * HEAD_DIM + 1]
        parts.append(mix[:HEAD_DIM, :width] * inverse[:, :width])
        parts.append(mix[HEAD_DIM : 2 * HEAD_DIM, width:] * inverse[:, width:])
    return jnp.concatenate(parts, axis=0).astype(BF16)


def query_stage(left, coarse, up_ref, wq_ref):
    up = nn(up_ref[...], coarse)
    query_in = (left.reshape(up.shape).astype(F32) + up).astype(BF16)
    return query_in, nt(wq_ref[...], query_in).astype(BF16)


def spread_queries(query_ref, spread_ref, start):
    for h in range(HEADS):
        rows = slice(h * HEAD_DIM, (h + 1) * HEAD_DIM)
        spread_ref[rows, h * BLOCK : (h + 1) * BLOCK] = query_ref[rows, pl.ds(start, BLOCK)]


def out_stage(query_in, mixed, wo_ref, gain_ref):
    product = tn(mixed, wo_ref[...])
    return layer_norm(query_in.astype(F32) + product, gain_ref[...]).astype(BF16)


def flipped(index, bit):
    return index + bit - 2 * bit * ((index // bit) % 2)


def gather_hops(n, me):
    if n != 8:
        return [(me, (me + j) % n, (me + n - j) % n, None) for j in range(1, n)]
    a, b, c = flipped(me, 1), flipped(me, 2), flipped(me, 4)
    d = flipped(b, 4)
    odd = me % 2
    relay_block = b + odd * (c - b)
    relay_target = c + odd * (b - c)
    return [
        (me, b, b, None),
        (me, c, c, None),
        (me, a, a, None),
        (relay_block, relay_target, d, (0, 1)),
        (b, a, flipped(b, 1), (0,)),
        (c, a, flipped(c, 1), (1,)),
        (d, a, flipped(d, 1), (3,)),
    ]


def gather_kernel(
    list_ref,
    count_ref,
    left_ref,
    right_ref,
    left_coarse_ref,
    right_coarse_ref,
    up_ref,
    wq_ref,
    wkv_ref,
    wo_ref,
    gain_ref,
    fold_ref,
    late_ref,
    fine_ref,
    prior_ref,
    ext_ref,
    *scratch,
    n,
    row_devices,
    early,
    length,
):
    bands_ref = scratch[:early]
    (
        coarse_ref,
        edge_low_ref,
        edge_high_ref,
        rows_ref,
        query_ref,
        spread_ref,
        mix_ref,
        coarse_send,
        coarse_recv,
        edge_send,
        edge_recv,
        fine_send,
        fine_recv,
        local_sem,
    ) = scratch[early:]
    me = lax.axis_index("cols")
    row = lax.axis_index("rows")
    bands = right_ref.shape[0] // BAND
    coarse_rows, coarse_cols, feat = left_coarse_ref.shape
    hops = gather_hops(n, me)

    barrier = pltpu.get_barrier_semaphore()
    for j in range(1, n):
        pl.semaphore_signal(
            barrier, inc=1, device_id={"cols": (me + j) % n}, device_id_type=MESH
        )

    @pl.when(row > 0)
    def _():
        pl.semaphore_signal(barrier, inc=1, device_id={"rows": row - 1}, device_id_type=MESH)

    @pl.when(row < row_devices - 1)
    def _():
        pl.semaphore_signal(barrier, inc=1, device_id={"rows": row + 1}, device_id_type=MESH)

    inner = (row > 0).astype(jnp.int32) + (row < row_devices - 1).astype(jnp.int32)
    pl.semaphore_wait(barrier, n - 1 + inner)

    def coarse_copy(j):
        return pltpu.make_async_remote_copy(
            src_ref=right_coarse_ref,
            dst_ref=coarse_ref.at[me],
            send_sem=coarse_send.at[j - 1],
            recv_sem=coarse_recv.at[j - 1],
            device_id={"cols": (me + j) % n},
            device_id_type=MESH,
        )

    def place(g, block):
        if g < early:
            return bands_ref[g].at[block]
        return late_ref.at[block, pl.ds((g - early) * BAND, BAND)]

    def fine_copy(g, hop):
        block, target, _, after = hops[hop]
        if after is None:
            source = right_ref.at[pl.ds(g * BAND, BAND)]
        else:
            source = place(g, block)
        return pltpu.make_async_remote_copy(
            src_ref=source,
            dst_ref=place(g, block),
            send_sem=fine_send.at[g, hop],
            recv_sem=fine_recv.at[g, hop],
            device_id={"cols": target},
            device_id_type=MESH,
        )

    def own_copy(g):
        return pltpu.make_async_copy(
            right_ref.at[pl.ds(g * BAND, BAND)], place(g, me), local_sem.at[g]
        )

    arrived = [set() for _ in range(bands)]

    def take(g, hop):
        if hop not in arrived[g]:
            arrived[g].add(hop)
            fine_copy(g, hop).wait_recv()

    levels = []
    for hop in hops:
        levels.append(0 if hop[3] is None else 1 + max(levels[i] for i in hop[3]))
    depth = max(levels)

    def send(g, level):
        for hop in range(len(hops)):
            if levels[hop] == level:
                for needed in hops[hop][3] or ():
                    take(g, needed)
                fine_copy(g, hop).start()

    ticks = []
    for t in range(1, bands + depth):
        ticks.append(
            [(t - level, level) for level in range(depth, 0, -1) if 0 <= t - level < bands]
            + ([(t + LEAD - 1, 0)] if t + LEAD - 1 < bands else [])
        )

    def tick():
        if ticks:
            for g, level in ticks.pop(0):
                send(g, level)

    for j in range(1, n):
        coarse_copy(j).start()
    for g in range(bands):
        own_copy(g).start()
    for g in range(min(LEAD, bands)):
        send(g, 0)

    spread_ref[...] = jnp.zeros_like(spread_ref)
    coarse_ref[me] = right_coarse_ref[...]
    for j in range(1, n):
        coarse_copy(j).wait()

    wide = HEADS * coarse_cols
    diagonal = (
        lax.broadcasted_iota(jnp.int32, (feat, wide), 0) // HEAD_DIM
        == lax.broadcasted_iota(jnp.int32, (feat, wide), 1) // coarse_cols
    )

    def coarse_row(r, carry):
        right = coarse_ref[:, r].reshape(n * coarse_cols, feat)
        left = left_coarse_ref[r]
        keys, values = project_blocks([right], wkv_ref)
        queries = nt(wq_ref[...], jnp.concatenate([left] * HEADS, axis=0))
        queries = jnp.where(diagonal, queries, 0.0).astype(BF16)
        scores = nn(keys, queries)
        top = jnp.max(scores, axis=0, keepdims=True)
        weights = jnp.exp2((scores - top).astype(BF16))
        total = jnp.sum(weights.astype(F32), axis=0, keepdims=True)
        mixed = nn(values, weights) * (1.0 / total)
        mixed = jnp.where(diagonal, mixed, 0.0).astype(BF16)
        folded = nt(fold_ref[...], mixed).astype(BF16)
        out = left.astype(F32) + nn(folded, wo_ref[...])
        out = layer_norm(out, gain_ref[...]).astype(BF16)
        rows_ref[r + 1] = out
        prior_ref[r] = out
        return carry

    lax.fori_loop(0, coarse_rows // 2, coarse_row, 0)
    tick()
    lax.fori_loop(coarse_rows // 2, coarse_rows, coarse_row, 0)

    def row_copy(up):
        return pltpu.make_async_remote_copy(
            src_ref=prior_ref.at[0 if up else coarse_rows - 1],
            dst_ref=rows_ref.at[coarse_rows + 1 if up else 0],
            send_sem=edge_send.at[0 if up else 1],
            recv_sem=edge_recv.at[0 if up else 1],
            device_id={"rows": row - 1 if up else row + 1},
            device_id_type=MESH,
        )

    def col_copy(left):
        return pltpu.make_async_remote_copy(
            src_ref=rows_ref.at[:, pl.ds(0 if left else coarse_cols - EDGE, EDGE)],
            dst_ref=edge_high_ref if left else edge_low_ref,
            send_sem=edge_send.at[2 if left else 3],
            recv_sem=edge_recv.at[2 if left else 3],
            device_id={"cols": me - 1 if left else me + 1},
            device_id_type=MESH,
        )

    has = (row > 0, row < row_devices - 1, me > 0, me < n - 1)

    @pl.when(has[0])
    def _():
        row_copy(True).start()

    @pl.when(has[1])
    def _():
        row_copy(False).start()

    @pl.when(has[0])
    def _():
        row_copy(False).wait_recv()
        row_copy(True).wait_send()

    @pl.when(jnp.logical_not(has[0]))
    def _():
        rows_ref[0] = rows_ref[1]

    @pl.when(has[1])
    def _():
        row_copy(True).wait_recv()
        row_copy(False).wait_send()

    @pl.when(jnp.logical_not(has[1]))
    def _():
        rows_ref[coarse_rows + 1] = rows_ref[coarse_rows]

    @pl.when(has[2])
    def _():
        col_copy(True).start()

    @pl.when(has[3])
    def _():
        col_copy(False).start()

    tick()

    @pl.when(has[2])
    def _():
        col_copy(False).wait_recv()
        col_copy(True).wait_send()

    @pl.when(jnp.logical_not(has[2]))
    def _():
        edge_low_ref[...] = jnp.broadcast_to(rows_ref[:, 0:1], edge_low_ref.shape)

    @pl.when(has[3])
    def _():
        col_copy(True).wait_recv()
        col_copy(False).wait_send()

    @pl.when(jnp.logical_not(has[3]))
    def _():
        edge_high_ref[...] = jnp.broadcast_to(
            rows_ref[:, coarse_cols - 1 : coarse_cols], edge_high_ref.shape
        )

    ext_ref[:, :EDGE] = edge_low_ref[...]
    ext_ref[:, EDGE : EDGE + coarse_cols] = rows_ref[...]
    ext_ref[:, EDGE + coarse_cols :] = edge_high_ref[...]

    for g in range(early):
        tick()
        own_copy(g).wait()
        for hop in range(len(hops)):
            take(g, hop)
        coarse = jnp.concatenate([ext_ref[g + i] for i in range(3)], axis=0)
        query_in, queries = query_stage(left_ref[g * BAND : (g + 1) * BAND], coarse, up_ref, wq_ref)
        query_ref[...] = queries
        used = count_ref[g]
        picks = [
            jnp.where(k < used, list_ref[g * length + k], list_ref[g * length])
            for k in range(length)
        ]
        lanes = lax.broadcasted_iota(jnp.int32, (1, length * BLOCK), 1)
        live = jnp.where(lanes < used * BLOCK, 1.0, 0.0).astype(BF16)

        def fine_row(r, carry, g=g, picks=picks, live=live):
            keys, values = project_blocks(
                [bands_ref[g][picks[k], r] for k in range(length)], wkv_ref
            )
            values = values * live
            ones = jnp.broadcast_to(live, (HEAD_DIM, live.shape[1]))
            start = pl.multiple_of(r * BLOCK, BLOCK)
            spread_queries(query_ref, spread_ref, start)
            mix_ref[:, pl.ds(start, BLOCK)] = attend(keys, values, ones, spread_ref)
            return carry

        lax.fori_loop(0, BAND // 2, fine_row, 0)
        tick()
        if g > 0:
            tick()
        lax.fori_loop(BAND // 2, BAND, fine_row, 0)
        out = out_stage(query_in, mix_ref[...], wo_ref, gain_ref)
        fine_ref[g * BAND : (g + 1) * BAND] = out.reshape(BAND, BLOCK, feat)

    while ticks:
        tick()
    for g in range(bands):
        if g >= early:
            own_copy(g).wait()
        for hop in range(len(hops)):
            take(g, hop)
            fine_copy(g, hop).wait_send()


def gather_stage(mesh_rows, n, left_fine, right_fine, left_coarse, right_coarse, lists, counts, w):
    rows, cols, feat = left_fine.shape
    bands = rows // BAND
    early = min(EARLY, bands - 1)
    coarse_rows, coarse_cols, _ = left_coarse.shape
    fold = np.tile(np.eye(coarse_cols, dtype=np.float32), (1, HEADS))
    hop_count = len(gather_hops(n, 0))
    vmem = pl.BlockSpec(memory_space=pltpu.VMEM)
    smem = pl.BlockSpec(memory_space=pltpu.SMEM)
    return pl.pallas_call(
        functools.partial(
            gather_kernel, n=n, row_devices=mesh_rows, early=early, length=lists.shape[1]
        ),
        out_shape=(
            jax.ShapeDtypeStruct((n, (bands - early) * BAND, cols, feat), BF16),
            jax.ShapeDtypeStruct((early * BAND, cols, feat), BF16),
            jax.ShapeDtypeStruct(left_coarse.shape, BF16),
            jax.ShapeDtypeStruct((coarse_rows + 2, coarse_cols + 2 * EDGE, feat), BF16),
        ),
        in_specs=[smem, smem] + [vmem] * 10,
        out_specs=(pl.BlockSpec(memory_space=pl.ANY), vmem, vmem, vmem),
        scratch_shapes=[pltpu.VMEM((n, BAND, cols, feat), BF16) for _ in range(early)]
        + [
            pltpu.VMEM((n,) + right_coarse.shape, BF16),
            pltpu.VMEM((coarse_rows + 2, EDGE, feat), BF16),
            pltpu.VMEM((coarse_rows + 2, EDGE, feat), BF16),
            pltpu.VMEM((coarse_rows + 2, coarse_cols, feat), BF16),
            pltpu.VMEM((feat, BAND * BLOCK), BF16),
            pltpu.VMEM((feat, HEADS * BLOCK), BF16),
            pltpu.VMEM((feat, BAND * BLOCK), BF16),
            pltpu.SemaphoreType.DMA((n - 1,)),
            pltpu.SemaphoreType.DMA((n - 1,)),
            pltpu.SemaphoreType.DMA((4,)),
            pltpu.SemaphoreType.DMA((4,)),
            pltpu.SemaphoreType.DMA((bands, hop_count)),
            pltpu.SemaphoreType.DMA((bands, hop_count)),
            pltpu.SemaphoreType.DMA((bands,)),
        ],
        compiler_params=pltpu.CompilerParams(collective_id=0, has_side_effects=True),
        name="gather_stage",
    )(
        lists.reshape(-1),
        counts,
        left_fine,
        right_fine,
        left_coarse,
        right_coarse,
        w["up"],
        w["wq"],
        w["wkv"],
        w["wo"],
        w["gain"],
        jnp.asarray(fold, BF16),
    )


def fine_kernel(
    list_ref,
    count_ref,
    left_ref,
    ext_ref,
    up_ref,
    wq_ref,
    wkv_ref,
    wo_ref,
    gain_ref,
    done_ref,
    *refs,
    early,
):
    list_length = len(refs) - 4
    cand_refs = refs[:list_length]
    out_ref, query_ref, spread_ref, mix_ref = refs[list_length:]
    band = pl.program_id(0)
    feat = wq_ref.shape[0]

    @pl.when(pl.program_id(0) == 0)
    def _():
        spread_ref[...] = jnp.zeros_like(spread_ref)

    @pl.when(band < early)
    def _():
        out_ref[...] = done_ref[...]

    @pl.when(band >= early)
    def _():
        coarse = jnp.concatenate([ext_ref[band + i] for i in range(3)], axis=0)
        query_in, queries = query_stage(left_ref[...], coarse, up_ref, wq_ref)
        query_ref[...] = queries

        for used in range(1, list_length + 1):

            @pl.when(count_ref[band] == used)
            def _():
                def row(r, carry):
                    keys, values = project_blocks(
                        [cand_refs[k][0, r] for k in range(used)], wkv_ref
                    )
                    ones = jnp.ones((HEAD_DIM, used * BLOCK), BF16)
                    start = pl.multiple_of(r * BLOCK, BLOCK)
                    spread_queries(query_ref, spread_ref, start)
                    mix_ref[:, pl.ds(start, BLOCK)] = attend(keys, values, ones, spread_ref)
                    return carry

                lax.fori_loop(0, BAND, row, 0)

        out_ref[...] = out_stage(query_in, mix_ref[...], wo_ref, gain_ref).reshape(out_ref.shape)


def fine_stage(left_fine, gathered, done, ext, lists, counts, w):
    rows, cols, feat = left_fine.shape
    bands = rows // BAND
    early = bands - gathered.shape[1] // BAND
    length = lists.shape[1]

    def whole(shape):
        return pl.BlockSpec(shape, lambda g, c, n: (0,) * len(shape))

    def picked(k):
        return pl.BlockSpec(
            (1, BAND, cols, feat),
            lambda g, c, n: (c[jnp.maximum(g, early) * length + k], jnp.maximum(g - early, 0), 0, 0),
        )

    def banded(index):
        return pl.BlockSpec((BAND, cols, feat), lambda g, c, n: (index(g), 0, 0))

    names = ("up", "wq", "wkv", "wo", "gain")
    return pl.pallas_call(
        functools.partial(fine_kernel, early=early),
        grid_spec=pltpu.PrefetchScalarGridSpec(
            num_scalar_prefetch=2,
            grid=(bands,),
            in_specs=[banded(lambda g: jnp.maximum(g, early)), whole(ext.shape)]
            + [whole(w[name].shape) for name in names]
            + [banded(lambda g: jnp.minimum(g, early - 1))]
            + [picked(k) for k in range(length)],
            out_specs=banded(lambda g: g),
            scratch_shapes=[
                pltpu.VMEM((feat, BAND * BLOCK), BF16),
                pltpu.VMEM((feat, HEADS * BLOCK), BF16),
                pltpu.VMEM((feat, BAND * BLOCK), BF16),
            ],
        ),
        out_shape=jax.ShapeDtypeStruct(left_fine.shape, BF16),
        name="fine_stage",
    )(
        lists.reshape(-1),
        counts,
        left_fine,
        ext,
        *[w[name] for name in names],
        done,
        *([gathered] * length),
    )


def body(
    left_fine,
    right_fine,
    left_coarse,
    right_coarse,
    candidates,
    counts,
    query_weight,
    key_weight,
    value_weight,
    out_weight,
    norm_gain,
):
    me = lax.axis_index("cols")
    lists = lax.dynamic_index_in_dim(candidates, me, 0, keepdims=False)
    own_counts = lax.dynamic_index_in_dim(counts, me, 0, keepdims=False)
    w = {
        "up": jnp.asarray(upsample_matrix(left_coarse.shape[1]), BF16),
        "wq": query_weight.T,
        "wkv": jnp.concatenate([key_weight, value_weight], axis=1),
        "wo": out_weight,
        "gain": norm_gain.reshape(1, -1),
    }
    gathered, done, coarse_prior, ext = gather_stage(
        lax.axis_size("rows"),
        lax.axis_size("cols"),
        left_fine,
        right_fine,
        left_coarse,
        right_coarse,
        lists,
        own_counts,
        w,
    )
    fine_features = fine_stage(left_fine, gathered, done, ext, lists, own_counts, w)
    return (fine_features, coarse_prior)


def solution(mesh):
    return jax.shard_map(
        body,
        mesh=mesh,
        in_specs=(
            P("rows", "cols", None),
            P("rows", "cols", None),
            P("rows", "cols", None),
            P("rows", "cols", None),
            P(None, "rows", None),
            P(None, "rows"),
            P(),
            P(),
            P(),
            P(),
            P(),
        ),
        out_specs=(P("rows", "cols", None), P("rows", "cols", None)),
        check_vma=False,
    )
```

```python
import functools
import math

import jax
import jax.numpy as jnp
import numpy as np
from jax import lax
from jax.experimental import pallas as pl
from jax.experimental.pallas import tpu as pltpu
from jax.sharding import PartitionSpec as P

HEADS = 8
HEAD_DIM = 16
BLOCK = 128
BAND = 4
EPSILON = 1e-05
PAIRS = HEADS // 2
EDGE = 16
EARLY = 6
LEAD = 4
MESH = pl.DeviceIdType.MESH
KEY_SCALE = math.log2(math.e) / math.sqrt(HEAD_DIM)
BF16 = jnp.bfloat16
F32 = jnp.float32


def nt(a, b):
    return lax.dot_general(a, b, (((1,), (1,)), ((), ())), preferred_element_type=F32)


def tn(a, b):
    return lax.dot_general(a, b, (((0,), (0,)), ((), ())), preferred_element_type=F32)


def nn(a, b):
    return jnp.dot(a, b, preferred_element_type=F32)


def layer_norm(values, norm_gain):
    average = jnp.mean(values, axis=-1, keepdims=True)
    centred = values - average
    spread = jnp.mean(centred * centred, axis=-1, keepdims=True)
    return centred * lax.rsqrt(spread + EPSILON) * norm_gain


def upsample_matrix(cols):
    taps = np.array(
        [[0.375, 0.625, 0.0], [0.125, 0.875, 0.0], [0.0, 0.875, 0.125], [0.0, 0.625, 0.375]]
    )
    pitch = cols + 2 * EDGE
    out = np.zeros((BAND, cols, 4, 3, pitch), np.float32)
    for c in range(cols):
        for t in range(4):
            for d in range(3):
                out[:, c, t, :, c + d + EDGE - 1] = taps[:, :] * taps[t, d]
    return out.reshape(BAND * cols * 4, 3 * pitch)


def project_blocks(blocks, wkv_ref):
    feat = blocks[0].shape[1]
    keys, values = [], []
    for block in blocks:
        both = nn(block, wkv_ref[...])
        keys.append((both[:, :feat] * KEY_SCALE).astype(BF16))
        values.append(both[:, feat:].astype(BF16).T)
    return jnp.concatenate(keys, axis=0), jnp.concatenate(values, axis=1)


def attend(keys, values, ones, spread_ref):
    parts = []
    width = spread_ref.shape[1] // HEADS

    def score(pair):
        return nn(keys, spread_ref[:, pair * 2 * width : (pair + 1) * 2 * width])

    ahead = score(0)
    for pair in range(PAIRS):
        scores = ahead
        if pair + 1 < PAIRS:
            ahead = score(pair + 1)
        top = jnp.max(scores, axis=0, keepdims=True)
        weights = jnp.exp2((scores - top).astype(BF16))
        rows = values[pair * 2 * HEAD_DIM : (pair + 1) * 2 * HEAD_DIM]
        mix = nn(jnp.concatenate([rows, ones], axis=0), weights)
        inverse = 1.0 / mix[2 * HEAD_DIM : 2 * HEAD_DIM + 1]
        parts.append(mix[:HEAD_DIM, :width] * inverse[:, :width])
        parts.append(mix[HEAD_DIM : 2 * HEAD_DIM, width:] * inverse[:, width:])
    return jnp.concatenate(parts, axis=0).astype(BF16)


def query_stage(left, coarse, up_ref, wq_ref):
    up = nn(up_ref[...], coarse)
    query_in = (left.reshape(up.shape).astype(F32) + up).astype(BF16)
    return query_in, nt(wq_ref[...], query_in).astype(BF16)


def spread_queries(query_ref, spread_ref, start):
    for h in range(HEADS):
        rows = slice(h * HEAD_DIM, (h + 1) * HEAD_DIM)
        spread_ref[rows, h * BLOCK : (h + 1) * BLOCK] = query_ref[rows, pl.ds(start, BLOCK)]


def out_stage(query_in, mixed, wo_ref, gain_ref):
    product = tn(mixed, wo_ref[...])
    return layer_norm(query_in.astype(F32) + product, gain_ref[...]).astype(BF16)


def flipped(index, bit):
    return index + bit - 2 * bit * ((index // bit) % 2)


def gather_hops(n, me):
    if n != 8:
        return [(me, (me + j) % n, (me + n - j) % n, None) for j in range(1, n)]
    a, b, c = flipped(me, 1), flipped(me, 2), flipped(me, 4)
    d = flipped(b, 4)
    odd = me % 2
    relay_block = b + odd * (c - b)
    relay_target = c + odd * (b - c)
    return [
        (me, b, b, None),
        (me, c, c, None),
        (me, a, a, None),
        (relay_block, relay_target, d, (0, 1)),
        (b, a, flipped(b, 1), (0,)),
        (c, a, flipped(c, 1), (1,)),
        (d, a, flipped(d, 1), (3,)),
    ]


def gather_kernel(
    list_ref,
    count_ref,
    left_ref,
    right_ref,
    left_coarse_ref,
    right_coarse_ref,
    up_ref,
    wq_ref,
    wkv_ref,
    wo_ref,
    gain_ref,
    fold_ref,
    late_ref,
    fine_ref,
    prior_ref,
    ext_ref,
    *scratch,
    n,
    row_devices,
    early,
    length,
):
    bands_ref = scratch[:early]
    (
        coarse_ref,
        edge_low_ref,
        edge_high_ref,
        rows_ref,
        query_ref,
        spread_ref,
        mix_ref,
        coarse_send,
        coarse_recv,
        edge_send,
        edge_recv,
        fine_send,
        fine_recv,
        local_sem,
    ) = scratch[early:]
    me = lax.axis_index("cols")
    row = lax.axis_index("rows")
    bands = right_ref.shape[0] // BAND
    coarse_rows, coarse_cols, feat = left_coarse_ref.shape
    hops = gather_hops(n, me)

    barrier = pltpu.get_barrier_semaphore()
    for j in range(1, n):
        pl.semaphore_signal(
            barrier, inc=1, device_id={"cols": (me + j) % n}, device_id_type=MESH
        )

    @pl.when(row > 0)
    def _():
        pl.semaphore_signal(barrier, inc=1, device_id={"rows": row - 1}, device_id_type=MESH)

    @pl.when(row < row_devices - 1)
    def _():
        pl.semaphore_signal(barrier, inc=1, device_id={"rows": row + 1}, device_id_type=MESH)

    inner = (row > 0).astype(jnp.int32) + (row < row_devices - 1).astype(jnp.int32)
    pl.semaphore_wait(barrier, n - 1 + inner)

    def coarse_copy(j):
        return pltpu.make_async_remote_copy(
            src_ref=right_coarse_ref,
            dst_ref=coarse_ref.at[me],
            send_sem=coarse_send.at[j - 1],
            recv_sem=coarse_recv.at[j - 1],
            device_id={"cols": (me + j) % n},
            device_id_type=MESH,
        )

    def place(g, block):
        if g < early:
            return bands_ref[g].at[block]
        return late_ref.at[block, pl.ds((g - early) * BAND, BAND)]

    def fine_copy(g, hop):
        block, target, _, after = hops[hop]
        if after is None:
            source = right_ref.at[pl.ds(g * BAND, BAND)]
        else:
            source = place(g, block)
        return pltpu.make_async_remote_copy(
            src_ref=source,
            dst_ref=place(g, block),
            send_sem=fine_send.at[g, hop],
            recv_sem=fine_recv.at[g, hop],
            device_id={"cols": target},
            device_id_type=MESH,
        )

    def own_copy(g):
        return pltpu.make_async_copy(
            right_ref.at[pl.ds(g * BAND, BAND)], place(g, me), local_sem.at[g]
        )

    arrived = [set() for _ in range(bands)]

    def take(g, hop):
        if hop not in arrived[g]:
            arrived[g].add(hop)
            fine_copy(g, hop).wait_recv()

    levels = []
    for hop in hops:
        levels.append(0 if hop[3] is None else 1 + max(levels[i] for i in hop[3]))
    depth = max(levels)

    def send(g, level):
        for hop in range(len(hops)):
            if levels[hop] == level:
                for needed in hops[hop][3] or ():
                    take(g, needed)
                fine_copy(g, hop).start()

    ticks = []
    for t in range(1, bands + depth):
        ticks.append(
            [(t - level, level) for level in range(depth, 0, -1) if 0 <= t - level < bands]
            + ([(t + LEAD - 1, 0)] if t + LEAD - 1 < bands else [])
        )

    def tick():
        if ticks:
            for g, level in ticks.pop(0):
                send(g, level)

    for j in range(1, n):
        coarse_copy(j).start()
    for g in range(bands):
        own_copy(g).start()
    for g in range(min(LEAD, bands)):
        send(g, 0)

    spread_ref[...] = jnp.zeros_like(spread_ref)
    coarse_ref[me] = right_coarse_ref[...]
    for j in range(1, n):
        coarse_copy(j).wait()

    wide = HEADS * coarse_cols
    diagonal = (
        lax.broadcasted_iota(jnp.int32, (feat, wide), 0) // HEAD_DIM
        == lax.broadcasted_iota(jnp.int32, (feat, wide), 1) // coarse_cols
    )

    def coarse_row(r, carry):
        right = coarse_ref[:, r].reshape(n * coarse_cols, feat)
        left = left_coarse_ref[r]
        keys, values = project_blocks([right], wkv_ref)
        queries = nt(wq_ref[...], jnp.concatenate([left] * HEADS, axis=0))
        queries = jnp.where(diagonal, queries, 0.0).astype(BF16)
        scores = nn(keys, queries)
        top = jnp.max(scores, axis=0, keepdims=True)
        weights = jnp.exp2((scores - top).astype(BF16))
        total = jnp.sum(weights.astype(F32), axis=0, keepdims=True)
        mixed = nn(values, weights) * (1.0 / total)
        mixed = jnp.where(diagonal, mixed, 0.0).astype(BF16)
        folded = nt(fold_ref[...], mixed).astype(BF16)
        out = left.astype(F32) + nn(folded, wo_ref[...])
        out = layer_norm(out, gain_ref[...]).astype(BF16)
        rows_ref[r + 1] = out
        prior_ref[r] = out
        return carry

    lax.fori_loop(0, coarse_rows // 2, coarse_row, 0)
    tick()
    lax.fori_loop(coarse_rows // 2, coarse_rows, coarse_row, 0)

    def row_copy(up):
        return pltpu.make_async_remote_copy(
            src_ref=prior_ref.at[0 if up else coarse_rows - 1],
            dst_ref=rows_ref.at[coarse_rows + 1 if up else 0],
            send_sem=edge_send.at[0 if up else 1],
            recv_sem=edge_recv.at[0 if up else 1],
            device_id={"rows": row - 1 if up else row + 1},
            device_id_type=MESH,
        )

    def col_copy(left):
        return pltpu.make_async_remote_copy(
            src_ref=rows_ref.at[:, pl.ds(0 if left else coarse_cols - EDGE, EDGE)],
            dst_ref=edge_high_ref if left else edge_low_ref,
            send_sem=edge_send.at[2 if left else 3],
            recv_sem=edge_recv.at[2 if left else 3],
            device_id={"cols": me - 1 if left else me + 1},
            device_id_type=MESH,
        )

    has = (row > 0, row < row_devices - 1, me > 0, me < n - 1)

    @pl.when(has[0])
    def _():
        row_copy(True).start()

    @pl.when(has[1])
    def _():
        row_copy(False).start()

    @pl.when(has[0])
    def _():
        row_copy(False).wait_recv()
        row_copy(True).wait_send()

    @pl.when(jnp.logical_not(has[0]))
    def _():
        rows_ref[0] = rows_ref[1]

    @pl.when(has[1])
    def _():
        row_copy(True).wait_recv()
        row_copy(False).wait_send()

    @pl.when(jnp.logical_not(has[1]))
    def _():
        rows_ref[coarse_rows + 1] = rows_ref[coarse_rows]

    @pl.when(has[2])
    def _():
        col_copy(True).start()

    @pl.when(has[3])
    def _():
        col_copy(False).start()

    tick()

    @pl.when(has[2])
    def _():
        col_copy(False).wait_recv()
        col_copy(True).wait_send()

    @pl.when(jnp.logical_not(has[2]))
    def _():
        edge_low_ref[...] = jnp.broadcast_to(rows_ref[:, 0:1], edge_low_ref.shape)

    @pl.when(has[3])
    def _():
        col_copy(True).wait_recv()
        col_copy(False).wait_send()

    @pl.when(jnp.logical_not(has[3]))
    def _():
        edge_high_ref[...] = jnp.broadcast_to(
            rows_ref[:, coarse_cols - 1 : coarse_cols], edge_high_ref.shape
        )

    ext_ref[:, :EDGE] = edge_low_ref[...]
    ext_ref[:, EDGE : EDGE + coarse_cols] = rows_ref[...]
    ext_ref[:, EDGE + coarse_cols :] = edge_high_ref[...]

    for g in range(early):
        if g == 0:
            tick()
        own_copy(g).wait()
        for hop in range(len(hops)):
            take(g, hop)
        coarse = jnp.concatenate([ext_ref[g + i] for i in range(3)], axis=0)
        query_in, queries = query_stage(left_ref[g * BAND : (g + 1) * BAND], coarse, up_ref, wq_ref)
        query_ref[...] = queries
        used = count_ref[g]
        picks = [
            jnp.where(k < used, list_ref[g * length + k], list_ref[g * length])
            for k in range(length)
        ]
        lanes = lax.broadcasted_iota(jnp.int32, (1, length * BLOCK), 1)
        live = jnp.where(lanes < used * BLOCK, 1.0, 0.0).astype(BF16)

        def fine_row(r, carry, g=g, picks=picks, live=live):
            keys, values = project_blocks(
                [bands_ref[g][picks[k], r] for k in range(length)], wkv_ref
            )
            values = values * live
            ones = jnp.broadcast_to(live, (HEAD_DIM, live.shape[1]))
            start = pl.multiple_of(r * BLOCK, BLOCK)
            spread_queries(query_ref, spread_ref, start)
            mix_ref[:, pl.ds(start, BLOCK)] = attend(keys, values, ones, spread_ref)
            return carry

        lax.fori_loop(0, BAND // 2, fine_row, 0)
        tick()
        lax.fori_loop(BAND // 2, BAND, fine_row, 0)
        out = out_stage(query_in, mix_ref[...], wo_ref, gain_ref)
        fine_ref[g * BAND : (g + 1) * BAND] = out.reshape(BAND, BLOCK, feat)

    while ticks:
        tick()
    for g in range(bands):
        if g >= early:
            own_copy(g).wait()
        for hop in range(len(hops)):
            take(g, hop)
            fine_copy(g, hop).wait_send()


def gather_stage(mesh_rows, n, left_fine, right_fine, left_coarse, right_coarse, lists, counts, w):
    rows, cols, feat = left_fine.shape
    bands = rows // BAND
    early = min(EARLY, bands - 1)
    coarse_rows, coarse_cols, _ = left_coarse.shape
    fold = np.tile(np.eye(coarse_cols, dtype=np.float32), (1, HEADS))
    hop_count = len(gather_hops(n, 0))
    vmem = pl.BlockSpec(memory_space=pltpu.VMEM)
    smem = pl.BlockSpec(memory_space=pltpu.SMEM)
    return pl.pallas_call(
        functools.partial(
            gather_kernel, n=n, row_devices=mesh_rows, early=early, length=lists.shape[1]
        ),
        out_shape=(
            jax.ShapeDtypeStruct((n, (bands - early) * BAND, cols, feat), BF16),
            jax.ShapeDtypeStruct((early * BAND, cols, feat), BF16),
            jax.ShapeDtypeStruct(left_coarse.shape, BF16),
            jax.ShapeDtypeStruct((coarse_rows + 2, coarse_cols + 2 * EDGE, feat), BF16),
        ),
        in_specs=[smem, smem] + [vmem] * 10,
        out_specs=(pl.BlockSpec(memory_space=pl.ANY), vmem, vmem, vmem),
        scratch_shapes=[pltpu.VMEM((n, BAND, cols, feat), BF16) for _ in range(early)]
        + [
            pltpu.VMEM((n,) + right_coarse.shape, BF16),
            pltpu.VMEM((coarse_rows + 2, EDGE, feat), BF16),
            pltpu.VMEM((coarse_rows + 2, EDGE, feat), BF16),
            pltpu.VMEM((coarse_rows + 2, coarse_cols, feat), BF16),
            pltpu.VMEM((feat, BAND * BLOCK), BF16),
            pltpu.VMEM((feat, HEADS * BLOCK), BF16),
            pltpu.VMEM((feat, BAND * BLOCK), BF16),
            pltpu.SemaphoreType.DMA((n - 1,)),
            pltpu.SemaphoreType.DMA((n - 1,)),
            pltpu.SemaphoreType.DMA((4,)),
            pltpu.SemaphoreType.DMA((4,)),
            pltpu.SemaphoreType.DMA((bands, hop_count)),
            pltpu.SemaphoreType.DMA((bands, hop_count)),
            pltpu.SemaphoreType.DMA((bands,)),
        ],
        compiler_params=pltpu.CompilerParams(collective_id=0, has_side_effects=True),
        name="gather_stage",
    )(
        lists.reshape(-1),
        counts,
        left_fine,
        right_fine,
        left_coarse,
        right_coarse,
        w["up"],
        w["wq"],
        w["wkv"],
        w["wo"],
        w["gain"],
        jnp.asarray(fold, BF16),
    )


def fine_kernel(
    list_ref,
    count_ref,
    left_ref,
    ext_ref,
    up_ref,
    wq_ref,
    wkv_ref,
    wo_ref,
    gain_ref,
    done_ref,
    *refs,
    early,
):
    list_length = len(refs) - 4
    cand_refs = refs[:list_length]
    out_ref, query_ref, spread_ref, mix_ref = refs[list_length:]
    band = pl.program_id(0)
    feat = wq_ref.shape[0]

    @pl.when(pl.program_id(0) == 0)
    def _():
        spread_ref[...] = jnp.zeros_like(spread_ref)

    @pl.when(band < early)
    def _():
        out_ref[...] = done_ref[...]

    @pl.when(band >= early)
    def _():
        coarse = jnp.concatenate([ext_ref[band + i] for i in range(3)], axis=0)
        query_in, queries = query_stage(left_ref[...], coarse, up_ref, wq_ref)
        query_ref[...] = queries

        for used in range(1, list_length + 1):

            @pl.when(count_ref[band] == used)
            def _():
                def row(r, carry):
                    keys, values = project_blocks(
                        [cand_refs[k][0, r] for k in range(used)], wkv_ref
                    )
                    ones = jnp.ones((HEAD_DIM, used * BLOCK), BF16)
                    start = pl.multiple_of(r * BLOCK, BLOCK)
                    spread_queries(query_ref, spread_ref, start)
                    mix_ref[:, pl.ds(start, BLOCK)] = attend(keys, values, ones, spread_ref)
                    return carry

                lax.fori_loop(0, BAND, row, 0)

        out_ref[...] = out_stage(query_in, mix_ref[...], wo_ref, gain_ref).reshape(out_ref.shape)


def fine_stage(left_fine, gathered, done, ext, lists, counts, w):
    rows, cols, feat = left_fine.shape
    bands = rows // BAND
    early = bands - gathered.shape[1] // BAND
    length = lists.shape[1]

    def whole(shape):
        return pl.BlockSpec(shape, lambda g, c, n: (0,) * len(shape))

    def picked(k):
        return pl.BlockSpec(
            (1, BAND, cols, feat),
            lambda g, c, n: (c[jnp.maximum(g, early) * length + k], jnp.maximum(g - early, 0), 0, 0),
        )

    def banded(index):
        return pl.BlockSpec((BAND, cols, feat), lambda g, c, n: (index(g), 0, 0))

    names = ("up", "wq", "wkv", "wo", "gain")
    return pl.pallas_call(
        functools.partial(fine_kernel, early=early),
        grid_spec=pltpu.PrefetchScalarGridSpec(
            num_scalar_prefetch=2,
            grid=(bands,),
            in_specs=[banded(lambda g: jnp.maximum(g, early)), whole(ext.shape)]
            + [whole(w[name].shape) for name in names]
            + [banded(lambda g: jnp.minimum(g, early - 1))]
            + [picked(k) for k in range(length)],
            out_specs=banded(lambda g: g),
            scratch_shapes=[
                pltpu.VMEM((feat, BAND * BLOCK), BF16),
                pltpu.VMEM((feat, HEADS * BLOCK), BF16),
                pltpu.VMEM((feat, BAND * BLOCK), BF16),
            ],
        ),
        out_shape=jax.ShapeDtypeStruct(left_fine.shape, BF16),
        name="fine_stage",
    )(
        lists.reshape(-1),
        counts,
        left_fine,
        ext,
        *[w[name] for name in names],
        done,
        *([gathered] * length),
    )


def body(
    left_fine,
    right_fine,
    left_coarse,
    right_coarse,
    candidates,
    counts,
    query_weight,
    key_weight,
    value_weight,
    out_weight,
    norm_gain,
):
    me = lax.axis_index("cols")
    lists = lax.dynamic_index_in_dim(candidates, me, 0, keepdims=False)
    own_counts = lax.dynamic_index_in_dim(counts, me, 0, keepdims=False)
    w = {
        "up": jnp.asarray(upsample_matrix(left_coarse.shape[1]), BF16),
        "wq": query_weight.T,
        "wkv": jnp.concatenate([key_weight, value_weight], axis=1),
        "wo": out_weight,
        "gain": norm_gain.reshape(1, -1),
    }
    gathered, done, coarse_prior, ext = gather_stage(
        lax.axis_size("rows"),
        lax.axis_size("cols"),
        left_fine,
        right_fine,
        left_coarse,
        right_coarse,
        lists,
        own_counts,
        w,
    )
    fine_features = fine_stage(left_fine, gathered, done, ext, lists, own_counts, w)
    return (fine_features, coarse_prior)


def solution(mesh):
    return jax.shard_map(
        body,
        mesh=mesh,
        in_specs=(
            P("rows", "cols", None),
            P("rows", "cols", None),
            P("rows", "cols", None),
            P("rows", "cols", None),
            P(None, "rows", None),
            P(None, "rows"),
            P(),
            P(),
            P(),
            P(),
            P(),
        ),
        out_specs=(P("rows", "cols", None), P("rows", "cols", None)),
        check_vma=False,
    )
```
